512 devices in a mesh: gx: 32 (over z, core), vert: 16 (over y, x).
Axes of the slice: x: 4, y: 4, z: 16, core: 2. Of those that a mesh axis runs over, the one named last changes fastest.
Arguments:
- distribution: float32 [4096, 32, 256], P('vert', 'gx'), may hold values from -6 to 6
- relax_rate: float32 [32, 256], P('gx'), may hold values from 0.3 to 3
- node_weight: float32 [4096], P('vert'), may hold values from 0.05 to 1
- kernel_tiles: bfloat16 [32, 128, 1536], P('vert'), may hold values from -0.15625 to 0.15625
- tile_cols: int32 [32, 12], P('vert'), may hold values from 0 to 31, as said below
Outputs:
- new_distribution: float32 [4096, 32, 256], P('vert', 'gx')
The draws below stay inside these ranges and needn't reach their ends.
Inputs may be any that keep to these rules, and one draw needn't show every extreme that they name: `tile_cols`: row block r lists its own block r first; the 12 column blocks listed for one row block are distinct.
All inputs are finite; a program needn't handle non-finite values.
Results may differ from the reference program's by a relative error of at most 0.0021.
Values may be sent and summed in bfloat16 or wider, within the bound.
No kernel may reach another device: no remote copies, remote signals or barrier semaphores. Data moves between devices by JAX's collectives and lax.ppermute only.
A program may use at most 64 MiB of HBM per device.

```python
import math
import jax
import jax.numpy as jnp
from jax import lax

Q = 16
TILE = 128
NB = 12
NZ = 4
STEPS = 2
V = 4096
RBLK = 32
NYZ = 256
NX = 32


def draw_tile_cols(key, part):
    row_ids = jnp.arange(RBLK, dtype=jnp.int32)
    row_keys = jax.random.split(key, RBLK)
    others = jax.vmap(lambda row_key: jax.random.permutation(row_key, RBLK - 1))(row_keys)
    others = others[:, :NB - 1].astype(jnp.int32)
    others = others + (others >= row_ids[:, None]).astype(jnp.int32)
    return jnp.concatenate([row_ids[:, None], others], axis=1)


def block_scale(stream_key, dims, cuts, least, largest):
    def one(position, parts):
        heights = jax.random.uniform(jax.random.fold_in(jax.random.fold_in(stream_key, 6), position), (parts,), jnp.float32, least / len(cuts), largest / len(cuts))
        return jnp.repeat(jnp.exp(heights), dims[position] // parts).reshape((-1,) + (1,) * (len(dims) - position - 1))

    level = one(*cuts[0])
    for cut in cuts[1:]:
        level = level * one(*cut)
    return level


def gaussian(own_key, extent, deviation, limit, shards=(), kind=jnp.bfloat16):
    drawn = deviation * jax.random.normal(own_key, extent, jnp.float32)
    if shards:
        drawn = drawn * block_scale(own_key, extent, shards, -0.22, 0.18)
    return jnp.clip(drawn, -limit, limit).astype(kind)


def setup_inputs(seed: int = 0) -> dict:
    streams_of = jax.random.split(jax.random.key(seed), 6)
    return {
        "distribution": gaussian(streams_of[0], (V, NX, NYZ), 1.0, 6.0, ((0, 16), (1, 32)), jnp.float32),
        "relax_rate": jnp.clip(jnp.exp(math.log(3.0) - 2.3025851 * jax.random.uniform(streams_of[1], (NX, NYZ), jnp.float32) ** block_scale(streams_of[1], (NX, NYZ), ((0, 32),), -0.2, 0.2)), 0.3, 3.0),
        "node_weight": jnp.clip(jnp.exp(math.log(1.0) - 2.9957323 * jax.random.uniform(streams_of[2], (V,), jnp.float32) ** block_scale(streams_of[2], (V,), ((0, 16),), -0.2, 0.2)), 0.05, 1.0),
        "kernel_tiles": gaussian(streams_of[3], (RBLK, TILE, NB * TILE), (NB * TILE) ** -0.5, 0.15625, ((0, 16),)),
        "tile_cols": draw_tile_cols(jax.random.fold_in(streams_of[5], 71), 0),
    }


COURANT_SCALE = 0.3
KERNEL_STEP = 0.5
PRECISE = lax.Precision.HIGHEST

def node_components(first_node, node_count):
    node_index = first_node + jnp.arange(node_count, dtype=jnp.int32)
    middle = (Q - 1) / 2.0
    speed_x = ((node_index % Q).astype(jnp.float32) - middle) / middle
    speed_y = ((node_index // Q % Q).astype(jnp.float32) - middle) / middle
    speed_z = ((node_index // (Q * Q)).astype(jnp.float32) - middle) / middle
    courant = COURANT_SCALE * jnp.stack([speed_x, speed_y, speed_z])
    squares = speed_x * speed_x + speed_y * speed_y + speed_z * speed_z
    invariants = jnp.stack([jnp.ones_like(speed_x), speed_x, speed_y, speed_z, squares])
    return (courant, invariants)

def gram_inverse(weighted, invariants):
    gram_matrix = jnp.dot(weighted, invariants.T, precision=PRECISE)
    factor = jnp.linalg.cholesky(gram_matrix)
    return jax.scipy.linalg.cho_solve((factor, True), jnp.eye(5, dtype=gram_matrix.dtype))

def advect(source, lower_x, upper_x, courant):
    plane_size = source.shape[-1]
    z_index = jnp.arange(plane_size, dtype=jnp.int32) % NZ
    lower_y = jnp.roll(source, NZ, axis=-1)
    upper_y = jnp.roll(source, -NZ, axis=-1)
    lower_z = jnp.where(z_index == 0, jnp.roll(source, 1 - NZ, axis=-1), jnp.roll(source, 1, axis=-1))
    upper_z = jnp.where(z_index == NZ - 1, jnp.roll(source, NZ - 1, axis=-1), jnp.roll(source, -1, axis=-1))
    total_flux = jnp.zeros_like(source)
    for component, below, above in ((0, lower_x, upper_x), (1, lower_y, upper_y), (2, lower_z, upper_z)):
        node_speed = courant[component][:, None, None]
        total_flux = total_flux + jnp.maximum(node_speed, 0.0) * (source - below) + jnp.minimum(node_speed, 0.0) * (above - source)
    return source - total_flux

def reference(distribution, relax_rate, node_weight, kernel_tiles, tile_cols):
    courant, invariants = node_components(0, V)
    weighted = invariants * node_weight[None, :]
    inverse = gram_inverse(weighted, invariants)
    relax_share = relax_rate / (1.0 + relax_rate)
    speed_blocks = courant.reshape(3, RBLK, TILE).transpose(1, 0, 2)
    current = distribution
    for step_index in range(STEPS):
        rounded = current.astype(jnp.bfloat16)
        blocks = rounded.reshape(RBLK, TILE, -1)
        cell_count = blocks.shape[-1]

        def block_update(block_pair):
            tile_row, column_list, source, speeds = block_pair
            picked = jnp.take(blocks, column_list, axis=0).reshape(-1, cell_count)
            kernel_term = jnp.dot(tile_row.astype(jnp.float32), picked.astype(jnp.float32), preferred_element_type=jnp.float32).reshape(source.shape)
            advected = advect(source, jnp.roll(source, 1, axis=1), jnp.roll(source, -1, axis=1), speeds)
            return advected + KERNEL_STEP * kernel_term
        explicit = lax.map(block_update, (kernel_tiles, tile_cols, current.reshape(RBLK, TILE, NX, -1), speed_blocks))
        explicit = explicit.reshape(current.shape)
        moments = jnp.dot(weighted, explicit.reshape(V, -1), precision=PRECISE)
        coeffs = jnp.dot(inverse, moments, precision=PRECISE)
        equilibrium = jnp.dot(invariants.T, coeffs, precision=PRECISE).reshape(current.shape)
        current = explicit - relax_share[None] * (explicit - equilibrium)
    return current
```

```python
import functools

import jax
import jax.numpy as jnp
from jax import lax
from jax.experimental import pallas as pl
from jax.experimental.pallas import tpu as pltpu
from jax.sharding import PartitionSpec as P

Q = 16
TILE = 128
NB = 12
NZ = 4
CELLS = 256
NODES = 256
PARTS = 16
COURANT_SCALE = 0.3
KERNEL_STEP = 0.5
MIDDLE = (Q - 1) / 2.0
EXTRA = 16
PAYLOAD = 32
GROUPS = 7
F32 = jnp.float32
BF16 = jnp.bfloat16
HIGHEST = lax.Precision.HIGHEST
VMEM_BYTES = 48 * 1024 * 1024


def iota(shape, dim):
    return lax.broadcasted_iota(jnp.int32, shape, dim)


def speed_of(index):
    return (index.astype(F32) - MIDDLE) / MIDDLE


def from_below_y(a):
    return pltpu.roll(a, NZ, 1)


def from_above_y(a):
    return pltpu.roll(a, CELLS - NZ, 1)


def from_below_z(a):
    first = iota(a.shape, 1) % NZ == 0
    return jnp.where(first, pltpu.roll(a, CELLS - (NZ - 1), 1), pltpu.roll(a, 1, 1))


def from_above_z(a):
    last = iota(a.shape, 1) % NZ == NZ - 1
    return jnp.where(last, pltpu.roll(a, NZ - 1, 1), pltpu.roll(a, CELLS - 1, 1))


def split(a, pieces):
    out = []
    for _ in range(pieces):
        out.append(a.astype(BF16))
        a = a - out[-1].astype(F32)
    return out


def three_sum(a):
    return a[0:8] + a[8:16] + a[16:24]


def node_rows(z_speed):
    node = iota((8, NODES), 1)
    k = iota((8, NODES), 0)
    x, y = speed_of(node % Q), speed_of(node // Q)
    z = jnp.full((8, NODES), z_speed)
    invariants = jnp.where(k == 0, 1.0, 0.0)
    for row, value in ((1, x), (2, y), (3, z), (4, x * x + y * y + z * z)):
        invariants = jnp.where(k == row, value, invariants)
    factors = [None]
    for speed in (x, y, z):
        factors.append(COURANT_SCALE * jnp.maximum(speed, 0.0))
        factors.append(COURANT_SCALE * jnp.maximum(-speed, 0.0))
    return invariants, factors


def kernel_product(gathered_ref, stride, tiles_ref, cols_ref, acc_ref):
    for r in range(2):
        blocks = []
        for j in range(NB):
            col = cols_ref[r, j]
            start = (col // 2) * stride + (col % 2) * TILE
            blocks.append(gathered_ref[pl.ds(pl.multiple_of(start, 16), TILE), :])
        acc_ref[r * TILE : (r + 1) * TILE, :] = jnp.dot(
            tiles_ref[r], jnp.concatenate(blocks, axis=0), preferred_element_type=F32
        )


def explicit_rows(m, s, below, above, kernel_term, z_speed):
    row = iota((Q, CELLS), 0)
    lane = iota((Q, CELLS), 1)
    x_courant = COURANT_SCALE * jnp.abs(speed_of(row))
    y_courant = COURANT_SCALE * abs((m - MIDDLE) / MIDDLE)
    z_courant = COURANT_SCALE * jnp.abs(z_speed)
    up = z_speed > 0
    edge = jnp.where(up, 0, NZ - 1)
    near = pltpu.roll(s, jnp.where(up, 1, CELLS - 1), 1)
    far = pltpu.roll(s, jnp.where(up, CELLS - (NZ - 1), NZ - 1), 1)
    z_side = jnp.where(lane % NZ == edge, far, near)
    y_side = from_below_y(s) if m >= Q // 2 else from_above_y(s)
    x_side = jnp.concatenate([above, below], axis=0)
    flux = x_courant * (s - x_side) + y_courant * (s - y_side) + z_courant * (s - z_side)
    return s - flux + KERNEL_STEP * kernel_term


def equilibrium_rows(m, coeffs, z_speed):
    y = (m - MIDDLE) / MIDDLE
    x = speed_of(iota((Q, CELLS), 0))
    common = coeffs[0:1] + y * coeffs[2:3] + z_speed * coeffs[3:4]
    common = common + (y * y + z_speed * z_speed) * coeffs[4:5]
    return common + x * coeffs[1:2] + (x * x) * coeffs[4:5]


def apply_small(matrix, first, rows):
    total = matrix[:, first : first + 1] * rows[0:1]
    for k in range(1, 5):
        total = total + matrix[:, first + k : first + k + 1] * rows[k : k + 1]
    return total


def inverse_of(gram):
    row, lane = iota((8, 128), 0), iota((8, 128), 1)
    work = jnp.where((row < 5) & (lane < 5), gram, 0.0)
    work = jnp.where((lane == row + 8) | ((lane == row) & (row >= 5)), 1.0, work)
    for i in range(5):
        pivot = work[i : i + 1, :] / work[i : i + 1, i : i + 1]
        work = jnp.where(row == i, pivot, work - work[:, i : i + 1] * pivot)
    return work


def load_state(ref, m):
    halves = [ref[pl.ds(2 * Q * m + h, Q, stride=2), :] for h in range(2)]
    return jnp.concatenate(halves, axis=1)


def store_sides(m, s, low_ref, high_ref):
    low_ref[8 * m : 8 * m + 8, :] = s[0:8]
    high_ref[8 * m : 8 * m + 8, :] = s[8:16]


def prologue_kernel(state_ref, copies_ref, low_ref, high_ref):
    for m in range(Q):
        s = load_state(state_ref, m)
        store_sides(m, s, low_ref, high_ref)
        rounded = s.astype(BF16)
        for part in range(PARTS):
            copies_ref[part * NODES + Q * m : part * NODES + Q * m + Q, :] = rounded


def first_kernel(
    cols_ref, z_ref, state_ref, rate_ref, weight_ref, tiles_ref, gathered_ref, above_ref, below_ref,
    scaled_ref, payload_ref, acc_ref, wk_ref,
):
    z_speed = z_ref[0]
    invariants, factors = node_rows(z_speed)
    base = weight_ref[...] * invariants
    phi = jnp.concatenate([base] + [base * f for f in factors[1:]], axis=0)
    kernel_product(gathered_ref, NODES, tiles_ref, cols_ref, acc_ref)
    keep = 1.0 / (1.0 + rate_ref[...])
    for m in range(Q):
        rows = slice(Q * m, Q * m + Q)
        half = slice(8 * m, 8 * m + 8)
        s = load_state(state_ref, m)
        e = explicit_rows(m, s, below_ref[half, :], above_ref[half, :], acc_ref[rows, :], z_speed)
        scaled_ref[rows, :] = keep * e
    moments = jnp.dot(phi, scaled_ref[...], precision=HIGHEST, preferred_element_type=F32)
    group = [moments[8 * t : 8 * t + 8] for t in range(GROUPS)]
    flux = group[1] + group[2]
    for t, shift in ((3, from_below_y), (4, from_above_y), (5, from_below_z), (6, from_above_z)):
        flux = flux + (group[t] - shift(group[t]))
    padded = jnp.concatenate([phi, jnp.zeros((TILE - 8 * GROUPS, NODES), F32)], axis=0)
    small = lax.dot_general(
        invariants, padded, (((1,), (1,)), ((), ())), precision=HIGHEST, preferred_element_type=F32
    )
    small = jnp.concatenate([small, jnp.zeros((8, CELLS - TILE), F32)], axis=1)
    wk_ref[...] = jnp.zeros_like(wk_ref)
    pieces = jnp.concatenate([p.astype(F32) for p in split(base, 3)], axis=0).astype(BF16)
    for r in range(2):
        part = three_sum(
            jnp.dot(pieces[:, r * TILE : (r + 1) * TILE], tiles_ref[r], preferred_element_type=F32)
        )
        for j in range(NB):
            col = cols_ref[r, j]
            wk_ref[col] = wk_ref[col] + part[:, j * TILE : (j + 1) * TILE]
    mine = iota((8, CELLS), 0) < 5
    third = jnp.where(mine, group[1], pltpu.roll(small, 5, 0))
    fourth = jnp.where(mine, group[2], pltpu.roll(small, 2, 0))
    for part in range(PARTS):
        wk = jnp.concatenate([wk_ref[2 * part], wk_ref[2 * part + 1]], axis=1)
        start = part * PAYLOAD
        payload_ref[start : start + 8, :] = jnp.where(mine, group[0], pltpu.roll(wk, 5, 0))
        payload_ref[start + 8 : start + 16, :] = jnp.where(mine, flux, pltpu.roll(wk, 2, 0))
        payload_ref[start + 16 : start + 24, :] = third
        payload_ref[start + 24 : start + 32, :] = fourth


def middle_kernel(
    z_ref, payload_ref, rate_ref, scaled_ref,
    state_ref, copies_ref, low_ref, high_ref, moments_ref, inverse_ref, rounded_ref,
):
    z_speed = z_ref[0]
    total = payload_ref[0:PAYLOAD, :]
    for part in range(1, PARTS):
        total = total + payload_ref[part * PAYLOAD : (part + 1) * PAYLOAD, :]
    group = [total[8 * t : 8 * t + 8] for t in range(4)]
    k = iota((8, CELLS), 0)
    mine = k < 5

    def spare(first, second):
        return jnp.where(
            k < 3, pltpu.roll(first, 3, 0), jnp.where(mine, pltpu.roll(second, 6, 0), 0.0)
        )

    wk = spare(group[0], group[1])
    small = spare(group[2], group[3])
    group = [jnp.where(mine, g, 0.0) for g in group]
    rate = rate_ref[...]
    share = rate / (1.0 + rate)
    inverse = inverse_of(small[:, 0:128])
    inverse_ref[...] = inverse
    coeffs = share * apply_small(inverse, 8, (1.0 + rate) * group[0])
    from_eq = [apply_small(small, 8 * t, coeffs) for t in range(GROUPS)]
    flux = group[1] + from_eq[1] + from_eq[2]
    for t, shift in ((3, from_below_y), (4, from_above_y), (5, from_below_z), (6, from_above_z)):
        flux = flux + (from_eq[t] - shift(from_eq[t]))
    moments_ref[...] = group[0] + from_eq[0] - flux
    high_ref[NODES // 2 :, :] = group[2] + from_eq[1]
    low_ref[NODES // 2 :, :] = group[3] + from_eq[2]
    for m in range(Q):
        rows = slice(Q * m, Q * m + Q)
        s = scaled_ref[rows, :] + equilibrium_rows(m, coeffs, z_speed)
        state_ref[rows, :] = s
        store_sides(m, s, low_ref, high_ref)
        rounded = s.astype(BF16)
        rounded_ref[rows, :] = rounded
        for part in range(PARTS):
            start = part * (NODES + EXTRA) + Q * m
            copies_ref[start : start + Q, :] = rounded
    pieces = jnp.concatenate([p.astype(F32) for p in split(wk, 3)], axis=0).astype(BF16)
    own = KERNEL_STEP * three_sum(jnp.dot(pieces, rounded_ref[...], preferred_element_type=F32))
    own = jnp.concatenate([p.astype(F32) for p in split(own, 2)], axis=0).astype(BF16)
    for part in range(PARTS):
        start = part * (NODES + EXTRA) + NODES
        copies_ref[start : start + EXTRA, :] = own


def last_kernel(
    cols_ref, z_ref, state_ref, rate_ref, tiles_ref, gathered_ref, above_ref, below_ref, moments_ref, inverse_ref,
    out_ref, acc_ref,
):
    z_speed = z_ref[0]
    kernel_product(gathered_ref, NODES + EXTRA, tiles_ref, cols_ref, acc_ref)
    total = moments_ref[...] + above_ref[NODES // 2 :, :] + below_ref[NODES // 2 :, :]
    for part in range(PARTS):
        start = part * (NODES + EXTRA) + NODES
        own = gathered_ref[start : start + EXTRA, :].astype(F32)
        total = total + (own[0:8] + own[8:16])
    rate = rate_ref[...]
    keep = 1.0 / (1.0 + rate)
    coeffs = rate * keep * apply_small(inverse_ref[...], 8, total)
    for m in range(Q):
        rows = slice(Q * m, Q * m + Q)
        half = slice(8 * m, 8 * m + 8)
        e = explicit_rows(
            m, state_ref[rows, :], below_ref[half, :], above_ref[half, :], acc_ref[rows, :], z_speed
        )
        new = keep * e + equilibrium_rows(m, coeffs, z_speed)
        for h in range(2):
            out_ref[pl.ds(2 * Q * m + h, Q, stride=2), :] = new[:, 128 * h : 128 * h + 128]


def call(kernel, scalars, arrays, outs, scratch=()):
    vmem = pl.BlockSpec(memory_space=pltpu.VMEM)
    smem = pl.BlockSpec(memory_space=pltpu.SMEM)
    return pl.pallas_call(
        kernel,
        out_shape=[jax.ShapeDtypeStruct(shape, kind) for shape, kind in outs],
        in_specs=[smem] * len(scalars) + [vmem] * len(arrays),
        out_specs=[vmem] * len(outs),
        scratch_shapes=[pltpu.VMEM(shape, kind) for shape, kind in scratch],
        compiler_params=pltpu.CompilerParams(vmem_limit_bytes=VMEM_BYTES),
    )(*scalars, *arrays)


def sides(low, high):
    count = lax.axis_size("gx")
    up = [(i, (i + 1) % count) for i in range(count)]
    down = [(target, source) for source, target in up]
    return lax.ppermute(low, "gx", down), lax.ppermute(high, "gx", up)


def spread(copies):
    return lax.all_to_all(copies, "vert", 0, 0, tiled=True)


def per_device(distribution, relax_rate, node_weight, kernel_tiles, tile_cols):
    state = distribution.reshape(2 * NODES, CELLS // 2)
    weight = node_weight.reshape(1, NODES)
    z_speed = speed_of(lax.axis_index("vert")).reshape(1)
    half = NODES // 2
    copies, low, high = call(
        prologue_kernel, [], [state],
        [((PARTS * NODES, CELLS), BF16), ((half, CELLS), F32), ((half, CELLS), F32)],
    )
    above, below = sides(low, high)
    gathered = spread(copies)
    scaled, payload = call(
        first_kernel, [tile_cols, z_speed],
        [state, relax_rate, weight, kernel_tiles, gathered, above, below],
        [((NODES, CELLS), F32), ((PARTS * PAYLOAD, CELLS), F32)],
        [((NODES, CELLS), F32), ((2 * PARTS, 8, TILE), F32)],
    )
    payload = spread(payload)
    state, copies, low, high, moments, inverse = call(
        middle_kernel, [z_speed], [payload, relax_rate, scaled],
        [
            ((NODES, CELLS), F32), ((PARTS * (NODES + EXTRA), CELLS), BF16), ((half + 8, CELLS), F32),
            ((half + 8, CELLS), F32), ((8, CELLS), F32), ((8, 128), F32),
        ],
        [((NODES, CELLS), BF16)],
    )
    above, below = sides(low, high)
    gathered = spread(copies)
    (out,) = call(
        last_kernel, [tile_cols, z_speed],
        [state, relax_rate, kernel_tiles, gathered, above, below, moments, inverse],
        [((2 * NODES, CELLS // 2), F32)],
        [((NODES, CELLS), F32)],
    )
    return out.reshape(distribution.shape)


def solution(mesh):
    placed = (
        P("vert", "gx", None),
        P("gx", None),
        P("vert"),
        P("vert", None, None),
        P("vert", None),
    )
    return jax.shard_map(
        per_device, mesh=mesh, in_specs=placed, out_specs=P("vert", "gx", None), check_vma=False
    )
```

```python
import functools

import jax
import jax.numpy as jnp
from jax import lax
from jax.experimental import pallas as pl
from jax.experimental.pallas import tpu as pltpu
from jax.sharding import PartitionSpec as P

Q = 16
TILE = 128
NB = 12
NZ = 4
CELLS = 256
NODES = 256
PARTS = 16
COURANT_SCALE = 0.3
KERNEL_STEP = 0.5
MIDDLE = (Q - 1) / 2.0
EXTRA = 16
PAYLOAD = 32
GROUPS = 7
F32 = jnp.float32
BF16 = jnp.bfloat16
HIGHEST = lax.Precision.HIGHEST
VMEM_BYTES = 24 * 1024 * 1024


def iota(shape, dim):
    return lax.broadcasted_iota(jnp.int32, shape, dim)


def speed_of(index):
    return (index.astype(F32) - MIDDLE) / MIDDLE


def from_below_y(a):
    return pltpu.roll(a, NZ, 1)


def from_above_y(a):
    return pltpu.roll(a, CELLS - NZ, 1)


def from_below_z(a):
    first = iota(a.shape, 1) % NZ == 0
    return jnp.where(first, pltpu.roll(a, CELLS - (NZ - 1), 1), pltpu.roll(a, 1, 1))


def from_above_z(a):
    last = iota(a.shape, 1) % NZ == NZ - 1
    return jnp.where(last, pltpu.roll(a, NZ - 1, 1), pltpu.roll(a, CELLS - 1, 1))


def split(a, pieces):
    out = []
    for _ in range(pieces):
        out.append(a.astype(BF16))
        a = a - out[-1].astype(F32)
    return out


def three_sum(a):
    return a[0:8] + a[8:16] + a[16:24]


def node_rows(z_speed):
    node = iota((8, NODES), 1)
    k = iota((8, NODES), 0)
    x, y = speed_of(node % Q), speed_of(node // Q)
    z = jnp.full((8, NODES), z_speed)
    invariants = jnp.where(k == 0, 1.0, 0.0)
    for row, value in ((1, x), (2, y), (3, z), (4, x * x + y * y + z * z)):
        invariants = jnp.where(k == row, value, invariants)
    factors = [None]
    for speed in (x, y, z):
        factors.append(COURANT_SCALE * jnp.maximum(speed, 0.0))
        factors.append(COURANT_SCALE * jnp.maximum(-speed, 0.0))
    return invariants, factors


def advected_rows(m, s, below, above, z_speed):
    row = iota((Q, CELLS), 0)
    lane = iota((Q, CELLS), 1)
    x_courant = COURANT_SCALE * jnp.abs(speed_of(row))
    y_courant = COURANT_SCALE * abs((m - MIDDLE) / MIDDLE)
    z_courant = COURANT_SCALE * jnp.abs(z_speed)
    up = z_speed > 0
    edge = jnp.where(up, 0, NZ - 1)
    near = pltpu.roll(s, jnp.where(up, 1, CELLS - 1), 1)
    far = pltpu.roll(s, jnp.where(up, CELLS - (NZ - 1), NZ - 1), 1)
    z_side = jnp.where(lane % NZ == edge, far, near)
    y_side = from_below_y(s) if m >= Q // 2 else from_above_y(s)
    x_side = jnp.concatenate([above, below], axis=0)
    flux = x_courant * (s - x_side) + y_courant * (s - y_side) + z_courant * (s - z_side)
    return s - flux


def equilibrium_rows(m, coeffs, z_speed):
    y = (m - MIDDLE) / MIDDLE
    x = speed_of(iota((Q, CELLS), 0))
    common = coeffs[0:1] + y * coeffs[2:3] + z_speed * coeffs[3:4]
    common = common + (y * y + z_speed * z_speed) * coeffs[4:5]
    return common + x * coeffs[1:2] + (x * x) * coeffs[4:5]


def apply_small(matrix, first, rows):
    total = matrix[:, first : first + 1] * rows[0:1]
    for k in range(1, 5):
        total = total + matrix[:, first + k : first + k + 1] * rows[k : k + 1]
    return total


def inverse_of(gram):
    row, lane = iota((8, 128), 0), iota((8, 128), 1)
    work = jnp.where((row < 5) & (lane < 5), gram, 0.0)
    work = jnp.where((lane == row + 8) | ((lane == row) & (row >= 5)), 1.0, work)
    for i in range(5):
        pivot = work[i : i + 1, :] / work[i : i + 1, i : i + 1]
        work = jnp.where(row == i, pivot, work - work[:, i : i + 1] * pivot)
    return work


def load_state(ref, m):
    halves = [ref[pl.ds(2 * Q * m + h, Q, stride=2), :] for h in range(2)]
    return jnp.concatenate(halves, axis=1)


def store_sides(m, s, low_ref, high_ref):
    low_ref[8 * m : 8 * m + 8, :] = s[0:8]
    high_ref[8 * m : 8 * m + 8, :] = s[8:16]


def in_parts(rows_per_part, start, block_ref, copies_ref, sems):
    count = block_ref.shape[0]
    copies = []
    for part in range(PARTS):
        at = part * rows_per_part + start
        copies.append(
            pltpu.make_async_copy(block_ref, copies_ref.at[at : at + count], sems.at[part])
        )
        copies[-1].start()
    return copies


def copies_kernel(state_ref, copies_ref, block_ref, sems):
    for m in range(Q):
        block_ref[Q * m : Q * m + Q, :] = load_state(state_ref, m).astype(BF16)
    for copy in in_parts(NODES, 0, block_ref, copies_ref, sems):
        copy.wait()


def prepare_kernel(
    cols_ref, z_ref, state_ref, weight_ref, tiles_ref,
    low_ref, high_ref, dense_ref, phi_ref, spare_ref, wk_ref,
):
    for m in range(Q):
        store_sides(m, load_state(state_ref, m), low_ref, high_ref)
    invariants, factors = node_rows(z_ref[0])
    base = weight_ref[...] * invariants
    phi = jnp.concatenate([base] + [base * f for f in factors[1:]], axis=0)
    phi_ref[...] = phi
    padded = jnp.concatenate([phi, jnp.zeros((TILE - 8 * GROUPS, NODES), F32)], axis=0)
    small = lax.dot_general(
        invariants, padded, (((1,), (1,)), ((), ())), precision=HIGHEST, preferred_element_type=F32
    )
    small = jnp.concatenate([small, jnp.zeros((8, CELLS - TILE), F32)], axis=1)
    dense_ref[...] = jnp.zeros_like(dense_ref)
    wk_ref[...] = jnp.zeros_like(wk_ref)
    pieces = jnp.concatenate([p.astype(F32) for p in split(base, 3)], axis=0).astype(BF16)
    for r in range(2):
        part = three_sum(
            jnp.dot(pieces[:, r * TILE : (r + 1) * TILE], tiles_ref[r], preferred_element_type=F32)
        )
        for j in range(NB):
            at = slice(j * TILE, (j + 1) * TILE)
            col = cols_ref[r, j]
            wk_ref[col] = wk_ref[col] + part[:, at]
            where = pl.ds(pl.multiple_of(col * TILE, TILE), TILE)
            dense_ref[r * TILE : (r + 1) * TILE, where] = tiles_ref[r, :, at]
    third = pltpu.roll(small, 5, 0)
    fourth = pltpu.roll(small, 2, 0)
    for part in range(PARTS):
        wk = jnp.concatenate([wk_ref[2 * part], wk_ref[2 * part + 1]], axis=1)
        start = part * PAYLOAD
        spare_ref[start : start + 8, :] = pltpu.roll(wk, 5, 0)
        spare_ref[start + 8 : start + 16, :] = pltpu.roll(wk, 2, 0)
        spare_ref[start + 16 : start + 24, :] = third
        spare_ref[start + 24 : start + 32, :] = fourth


def step_rows(rate, z_speed):
    keep = 1.0 / (1.0 + rate)
    rows = [KERNEL_STEP * keep, rate * keep, 1.0 + rate, jnp.full((1, CELLS), z_speed)]
    return jnp.concatenate(rows + [jnp.zeros((4, CELLS), F32)], axis=0)


def base_kernel(z_ref, state_ref, rate_ref, above_ref, below_ref, base_ref):
    z_speed = z_ref[0]
    rate = rate_ref[...]
    keep = 1.0 / (1.0 + rate)
    for m in range(Q):
        half = slice(8 * m, 8 * m + 8)
        s = load_state(state_ref, m)
        e = advected_rows(m, s, below_ref[half, :], above_ref[half, :], z_speed)
        base_ref[Q * m : Q * m + Q, :] = keep * e
    base_ref[NODES:, :] = step_rows(rate, z_speed)


def first_kernel(dense_ref, gathered_ref, base_ref, phi_ref, spare_ref, scaled_ref, payload_ref):
    term = jnp.dot(dense_ref[...], gathered_ref[...], preferred_element_type=F32)
    scaled = base_ref[0:NODES, :] + base_ref[NODES : NODES + 1, :] * term
    scaled_ref[0:NODES, :] = scaled
    scaled_ref[NODES:, :] = base_ref[NODES:, :]
    moments = jnp.dot(phi_ref[...], scaled, precision=HIGHEST, preferred_element_type=F32)
    group = [moments[8 * t : 8 * t + 8] for t in range(GROUPS)]
    flux = group[1] + group[2]
    for t, shift in ((3, from_below_y), (4, from_above_y), (5, from_below_z), (6, from_above_z)):
        flux = flux + (group[t] - shift(group[t]))
    mine = iota((8, CELLS), 0) < 5
    rows = (group[0], flux, group[1], group[2])
    for part in range(PARTS):
        for t in range(4):
            at = slice(part * PAYLOAD + 8 * t, part * PAYLOAD + 8 * t + 8)
            payload_ref[at, :] = jnp.where(mine, rows[t], spare_ref[at, :])


def totals_of(payload_ref, scaled_ref):
    total = payload_ref[0:PAYLOAD, :]
    for part in range(1, PARTS):
        total = total + payload_ref[part * PAYLOAD : (part + 1) * PAYLOAD, :]
    group = [total[8 * t : 8 * t + 8] for t in range(4)]
    k = iota((8, CELLS), 0)
    mine = k < 5

    def spare(first, second):
        return jnp.where(
            k < 3, pltpu.roll(first, 3, 0), jnp.where(mine, pltpu.roll(second, 6, 0), 0.0)
        )

    wk = spare(group[0], group[1])
    small = spare(group[2], group[3])
    group = [jnp.where(mine, g, 0.0) for g in group]
    inverse = inverse_of(small[:, 0:128])
    rows = scaled_ref[NODES:, :]
    coeffs = rows[1:2] * apply_small(inverse, 8, rows[2:3] * group[0])
    return group, wk, small, inverse, coeffs


def middle_kernel(payload_ref, scaled_ref, copies_ref, block_ref, own_ref, sems, own_sems):
    group, wk, small, inverse, coeffs = totals_of(payload_ref, scaled_ref)
    z_speed = scaled_ref[NODES + 3 : NODES + 4, :]
    for m in range(Q):
        rows = slice(Q * m, Q * m + Q)
        s = scaled_ref[rows, :] + equilibrium_rows(m, coeffs, z_speed)
        block_ref[rows, :] = s.astype(BF16)
    copies = in_parts(NODES + EXTRA, 0, block_ref, copies_ref, sems)
    pieces = jnp.concatenate([p.astype(F32) for p in split(wk, 3)], axis=0).astype(BF16)
    own = KERNEL_STEP * three_sum(jnp.dot(pieces, block_ref[...], preferred_element_type=F32))
    own_ref[...] = jnp.concatenate([p.astype(F32) for p in split(own, 2)], axis=0).astype(BF16)
    copies += in_parts(NODES + EXTRA, NODES, own_ref, copies_ref, own_sems)
    for copy in copies:
        copy.wait()


def state_kernel(payload_ref, scaled_ref, state_ref, low_ref, high_ref):
    group, wk, small, inverse, coeffs = totals_of(payload_ref, scaled_ref)
    z_speed = scaled_ref[NODES + 3 : NODES + 4, :]
    from_eq = [apply_small(small, 8 * t, coeffs) for t in range(GROUPS)]
    flux = group[1] + from_eq[1] + from_eq[2]
    for t, shift in ((3, from_below_y), (4, from_above_y), (5, from_below_z), (6, from_above_z)):
        flux = flux + (from_eq[t] - shift(from_eq[t]))
    high_ref[NODES // 2 :, :] = group[2] + from_eq[1]
    low_ref[NODES // 2 :, :] = group[3] + from_eq[2]
    for m in range(Q):
        rows = slice(Q * m, Q * m + Q)
        s = scaled_ref[rows, :] + equilibrium_rows(m, coeffs, z_speed)
        state_ref[rows, :] = s
        store_sides(m, s, low_ref, high_ref)
    state_ref[NODES : NODES + 8, :] = group[0] + from_eq[0] - flux
    state_ref[NODES + 8 :, :] = jnp.concatenate([inverse, inverse], axis=1)


def second_base_kernel(z_ref, state_ref, rate_ref, above_ref, below_ref, base_ref):
    z_speed = z_ref[0]
    rate = rate_ref[...]
    keep = 1.0 / (1.0 + rate)
    for m in range(Q):
        rows = slice(Q * m, Q * m + Q)
        half = slice(8 * m, 8 * m + 8)
        e = advected_rows(m, state_ref[rows, :], below_ref[half, :], above_ref[half, :], z_speed)
        base_ref[rows, :] = keep * e
    sides_part = above_ref[NODES // 2 :, :] + below_ref[NODES // 2 :, :]
    base_ref[NODES : NODES + 8, :] = state_ref[NODES : NODES + 8, :] + sides_part
    base_ref[NODES + 8 : NODES + 16, :] = state_ref[NODES + 8 : NODES + 16, :]
    base_ref[NODES + 16 :, :] = step_rows(rate, z_speed)


def last_kernel(dense_ref, gathered_ref, base_ref, out_ref, term_ref):
    stride = NODES + EXTRA
    term_ref[...] = jnp.dot(
        dense_ref[...],
        jnp.concatenate([gathered_ref[p * stride : p * stride + NODES, :] for p in range(PARTS)], axis=0),
        preferred_element_type=F32,
    )
    total = base_ref[NODES : NODES + 8, :]
    for part in range(PARTS):
        own = gathered_ref[part * stride + NODES : (part + 1) * stride, :].astype(F32)
        total = total + (own[0:8] + own[8:16])
    rows = base_ref[NODES + 16 :, :]
    coeffs = rows[1:2] * apply_small(base_ref[NODES + 8 : NODES + 16, 0:128], 8, total)
    for m in range(Q):
        at = slice(Q * m, Q * m + Q)
        new = base_ref[at, :] + rows[0:1] * term_ref[at, :] + equilibrium_rows(m, coeffs, rows[3:4])
        for h in range(2):
            out_ref[pl.ds(2 * Q * m + h, Q, stride=2), :] = new[:, 128 * h : 128 * h + 128]


VMEM = pl.BlockSpec(memory_space=pltpu.VMEM)
SMEM = pl.BlockSpec(memory_space=pltpu.SMEM)
ANY = pl.BlockSpec(memory_space=pl.ANY)


def call(kernel, scalars, arrays, outs, scratch=(), in_hbm=False):
    make = pltpu.HBM if in_hbm else jax.ShapeDtypeStruct
    return pl.pallas_call(
        kernel,
        out_shape=[make(shape, kind) for shape, kind in outs],
        in_specs=[SMEM] * len(scalars) + [VMEM] * len(arrays),
        out_specs=[ANY if in_hbm else VMEM] * len(outs),
        scratch_shapes=list(scratch),
        compiler_params=pltpu.CompilerParams(vmem_limit_bytes=VMEM_BYTES),
    )(*scalars, *arrays)


def sides(low, high):
    count = lax.axis_size("gx")
    up = [(i, (i + 1) % count) for i in range(count)]
    down = [(target, source) for source, target in up]
    return lax.ppermute(low, "gx", down), lax.ppermute(high, "gx", up)


def spread(copies):
    return lax.all_to_all(copies, "vert", 0, 0, tiled=True)


def per_device(distribution, relax_rate, node_weight, kernel_tiles, tile_cols):
    state = distribution.reshape(2 * NODES, CELLS // 2)
    weight = node_weight.reshape(1, NODES)
    z_speed = speed_of(lax.axis_index("vert")).reshape(1)
    half = NODES // 2
    block = pltpu.VMEM((NODES, CELLS), BF16)
    sems = pltpu.SemaphoreType.DMA((PARTS,))
    (copies,) = call(
        copies_kernel, [], [state], [((PARTS * NODES, CELLS), BF16)], [block, sems], True
    )
    gathered = spread(copies)
    low, high, dense, phi, spare = call(
        prepare_kernel, [tile_cols, z_speed], [state, weight, kernel_tiles],
        [
            ((half, CELLS), F32), ((half, CELLS), F32), ((NODES, PARTS * NODES), BF16),
            ((8 * GROUPS, NODES), F32), ((PARTS * PAYLOAD, CELLS), F32),
        ],
        [pltpu.VMEM((2 * PARTS, 8, TILE), F32)],
    )
    above, below = sides(low, high)
    (base,) = call(
        base_kernel, [z_speed], [state, relax_rate, above, below], [((NODES + 8, CELLS), F32)]
    )
    scaled, payload = call(
        first_kernel, [], [dense, gathered, base, phi, spare],
        [((NODES + 8, CELLS), F32), ((PARTS * PAYLOAD, CELLS), F32)],
    )
    payload = spread(payload)
    (copies,) = call(
        middle_kernel, [], [payload, scaled], [((PARTS * (NODES + EXTRA), CELLS), BF16)],
        [block, pltpu.VMEM((EXTRA, CELLS), BF16), sems, sems], True,
    )
    gathered = spread(copies)
    state, low, high = call(
        state_kernel, [], [payload, scaled],
        [((NODES + 16, CELLS), F32), ((half + 8, CELLS), F32), ((half + 8, CELLS), F32)],
    )
    above, below = sides(low, high)
    (base,) = call(
        second_base_kernel, [z_speed], [state, relax_rate, above, below],
        [((NODES + 24, CELLS), F32)],
    )
    (out,) = call(
        last_kernel, [], [dense, gathered, base], [((2 * NODES, CELLS // 2), F32)],
        [pltpu.VMEM((NODES, CELLS), F32)],
    )
    return out.reshape(distribution.shape)


def solution(mesh):
    placed = (
        P("vert", "gx", None),
        P("gx", None),
        P("vert"),
        P("vert", None, None),
        P("vert", None),
    )
    return jax.shard_map(
        per_device, mesh=mesh, in_specs=placed, out_specs=P("vert", "gx", None), check_vma=False
    )
```

```python
import functools

import jax
import jax.numpy as jnp
from jax import lax
from jax.experimental import pallas as pl
from jax.experimental.pallas import tpu as pltpu
from jax.sharding import PartitionSpec as P

Q = 16
TILE = 128
NB = 12
NZ = 4
CELLS = 256
NODES = 256
PARTS = 16
COURANT_SCALE = 0.3
KERNEL_STEP = 0.5
MIDDLE = (Q - 1) / 2.0
EXTRA = 16
PAYLOAD = 24
PIECES = 2
GROUPS = 7
F32 = jnp.float32
BF16 = jnp.bfloat16
HIGHEST = lax.Precision.HIGHEST
VMEM_BYTES = 24 * 1024 * 1024


def iota(shape, dim):
    return lax.broadcasted_iota(jnp.int32, shape, dim)


def speed_of(index):
    return (index.astype(F32) - MIDDLE) / MIDDLE


def from_below_y(a):
    return pltpu.roll(a, NZ, 1)


def from_above_y(a):
    return pltpu.roll(a, CELLS - NZ, 1)


def from_below_z(a):
    first = iota(a.shape, 1) % NZ == 0
    return jnp.where(first, pltpu.roll(a, CELLS - (NZ - 1), 1), pltpu.roll(a, 1, 1))


def from_above_z(a):
    last = iota(a.shape, 1) % NZ == NZ - 1
    return jnp.where(last, pltpu.roll(a, NZ - 1, 1), pltpu.roll(a, CELLS - 1, 1))


def split(a, pieces):
    out = []
    for _ in range(pieces):
        out.append(a.astype(BF16))
        a = a - out[-1].astype(F32)
    return out


def three_sum(a):
    return a[0:8] + a[8:16] + a[16:24]


def node_rows(z_speed):
    node = iota((8, NODES), 1)
    k = iota((8, NODES), 0)
    x, y = speed_of(node % Q), speed_of(node // Q)
    z = jnp.full((8, NODES), z_speed)
    invariants = jnp.where(k == 0, 1.0, 0.0)
    for row, value in ((1, x), (2, y), (3, z), (4, x * x + y * y + z * z)):
        invariants = jnp.where(k == row, value, invariants)
    factors = [None]
    for speed in (x, y, z):
        factors.append(COURANT_SCALE * jnp.maximum(speed, 0.0))
        factors.append(COURANT_SCALE * jnp.maximum(-speed, 0.0))
    return invariants, factors


def advected_rows(m, s, below, above, z_speed):
    row = iota((Q, CELLS), 0)
    lane = iota((Q, CELLS), 1)
    x_courant = COURANT_SCALE * jnp.abs(speed_of(row))
    y_courant = COURANT_SCALE * abs((m - MIDDLE) / MIDDLE)
    z_courant = COURANT_SCALE * jnp.abs(z_speed)
    up = z_speed > 0
    edge = jnp.where(up, 0, NZ - 1)
    near = pltpu.roll(s, jnp.where(up, 1, CELLS - 1), 1)
    far = pltpu.roll(s, jnp.where(up, CELLS - (NZ - 1), NZ - 1), 1)
    z_side = jnp.where(lane % NZ == edge, far, near)
    y_side = from_below_y(s) if m >= Q // 2 else from_above_y(s)
    x_side = jnp.concatenate([above, below], axis=0)
    flux = x_courant * (s - x_side) + y_courant * (s - y_side) + z_courant * (s - z_side)
    return s - flux


def equilibrium_rows(m, coeffs, z_speed):
    y = (m - MIDDLE) / MIDDLE
    x = speed_of(iota((Q, CELLS), 0))
    common = coeffs[0:1] + y * coeffs[2:3] + z_speed * coeffs[3:4]
    common = common + (y * y + z_speed * z_speed) * coeffs[4:5]
    return common + x * coeffs[1:2] + (x * x) * coeffs[4:5]


def apply_small(matrix, first, rows):
    total = matrix[:, first : first + 1] * rows[0:1]
    for k in range(1, 5):
        total = total + matrix[:, first + k : first + k + 1] * rows[k : k + 1]
    return total


def inverse_of(gram):
    row, lane = iota((8, 128), 0), iota((8, 128), 1)
    work = jnp.where((row < 5) & (lane < 5), gram, 0.0)
    work = jnp.where((lane == row + 8) | ((lane == row) & (row >= 5)), 1.0, work)
    for i in range(5):
        pivot = work[i : i + 1, :] / work[i : i + 1, i : i + 1]
        work = jnp.where(row == i, pivot, work - work[:, i : i + 1] * pivot)
    return work


def load_state(ref, m):
    halves = [ref[pl.ds(2 * Q * m + h, Q, stride=2), :] for h in range(2)]
    return jnp.concatenate(halves, axis=1)


def store_sides(m, s, low_ref, high_ref):
    low_ref[8 * m : 8 * m + 8, :] = s[0:8]
    high_ref[8 * m : 8 * m + 8, :] = s[8:16]


def in_parts(rows_per_part, start, piece, pieces, block_ref, copies_ref, sems):
    count = block_ref.shape[0] // pieces
    copies = []
    for part in range(PARTS):
        at = part * rows_per_part + start + piece * count
        copies.append(
            pltpu.make_async_copy(
                block_ref.at[piece * count : (piece + 1) * count],
                copies_ref.at[at : at + count],
                sems.at[piece, part],
            )
        )
        copies[-1].start()
    return copies


def copies_kernel(state_ref, copies_ref, held_ref, block_ref, in_sems, sems):
    pieces = []
    for i in range(PIECES):
        at = pl.ds(i * 2 * NODES // PIECES, 2 * NODES // PIECES)
        pieces.append(pltpu.make_async_copy(state_ref.at[at], held_ref.at[at], in_sems.at[i]))
        pieces[-1].start()
    copies = []
    for i in range(PIECES):
        pieces[i].wait()
        for m in range(i * Q // PIECES, (i + 1) * Q // PIECES):
            block_ref[Q * m : Q * m + Q, :] = load_state(held_ref, m).astype(BF16)
        copies += in_parts(NODES, 0, i, PIECES, block_ref, copies_ref, sems)
    for copy in copies:
        copy.wait()


def prepare_kernel(
    cols_ref, z_ref, state_ref, weight_ref, tiles_ref,
    low_ref, high_ref, dense_ref, phi_ref, wk_ref,
):
    for m in range(Q):
        store_sides(m, load_state(state_ref, m), low_ref, high_ref)
    invariants, factors = node_rows(z_ref[0])
    base = weight_ref[...] * invariants
    phi = jnp.concatenate([base] + [base * f for f in factors[1:]], axis=0)
    phi_ref[0 : 8 * GROUPS, :] = phi
    padded = jnp.concatenate([phi, jnp.zeros((TILE - 8 * GROUPS, NODES), F32)], axis=0)
    small = lax.dot_general(
        invariants, padded, (((1,), (1,)), ((), ())), precision=HIGHEST, preferred_element_type=F32
    )
    phi_ref[8 * GROUPS :, :] = jnp.concatenate([small, jnp.zeros((8, CELLS - TILE), F32)], axis=1)
    dense_ref[...] = jnp.zeros_like(dense_ref)
    wk_ref[...] = jnp.zeros_like(wk_ref)
    pieces = jnp.concatenate([p.astype(F32) for p in split(base, 3)], axis=0).astype(BF16)
    for r in range(2):
        part = three_sum(
            jnp.dot(pieces[:, r * TILE : (r + 1) * TILE], tiles_ref[r], preferred_element_type=F32)
        )
        for j in range(NB):
            at = slice(j * TILE, (j + 1) * TILE)
            col = cols_ref[r, j]
            wk_ref[col] = wk_ref[col] + part[:, at]
            where = pl.ds(pl.multiple_of(col * TILE, TILE), TILE)
            dense_ref[r * TILE : (r + 1) * TILE, where] = tiles_ref[r, :, at]


def step_rows(rate, z_speed):
    keep = 1.0 / (1.0 + rate)
    rows = [KERNEL_STEP * keep, rate * keep, 1.0 + rate, jnp.full((1, CELLS), z_speed)]
    return jnp.concatenate(rows + [jnp.zeros((4, CELLS), F32)], axis=0)


def base_kernel(z_ref, state_ref, rate_ref, above_ref, below_ref, base_ref):
    z_speed = z_ref[0]
    rate = rate_ref[...]
    keep = 1.0 / (1.0 + rate)
    for m in range(Q):
        half = slice(8 * m, 8 * m + 8)
        s = load_state(state_ref, m)
        e = advected_rows(m, s, below_ref[half, :], above_ref[half, :], z_speed)
        base_ref[Q * m : Q * m + Q, :] = keep * e
    base_ref[NODES:, :] = step_rows(rate, z_speed)


def fetch(gathered_ref, stride, held_ref, sems):
    copies = []
    for part in range(PARTS):
        at = slice(part * NODES, (part + 1) * NODES)
        source = gathered_ref.at[part * stride : part * stride + NODES]
        copies.append(pltpu.make_async_copy(source, held_ref.at[at], sems.at[part]))
        copies[-1].start()
    return copies


def product(dense_ref, held_ref, copies):
    total = None
    for i in range(4):
        for copy in copies[4 * i : 4 * i + 4]:
            copy.wait()
        at = slice(4 * i * NODES, 4 * (i + 1) * NODES)
        part = jnp.dot(dense_ref[:, at], held_ref[at, :], preferred_element_type=F32)
        total = part if total is None else total + part
    return total


def first_kernel(
    dense_ref, base_ref, phi_ref, wk_ref, gathered_ref, scaled_ref, payload_ref, held_ref, sems
):
    term = product(dense_ref, held_ref, fetch(gathered_ref, NODES, held_ref, sems))
    scaled = base_ref[0:NODES, :] + base_ref[NODES : NODES + 1, :] * term
    scaled_ref[0:NODES, :] = scaled
    scaled_ref[NODES : NODES + 8, :] = base_ref[NODES:, :]
    phi = phi_ref[0 : 8 * GROUPS, :]
    moments = jnp.dot(phi, scaled, precision=HIGHEST, preferred_element_type=F32)
    group = [moments[8 * t : 8 * t + 8] for t in range(GROUPS)]
    flux = group[1] + group[2]
    for t, shift in ((3, from_below_y), (4, from_above_y), (5, from_below_z), (6, from_above_z)):
        flux = flux + (group[t] - shift(group[t]))
    scaled_ref[NODES + 8 :, :] = flux
    k = iota((8, CELLS), 0)
    first = group[0]
    second = jnp.where(k < 5, group[1], pltpu.roll(group[2], 6, 0))
    third = jnp.where(k < 5, phi_ref[8 * GROUPS :, :], pltpu.roll(group[2], 3, 0))
    for part in range(PARTS):
        wk = jnp.concatenate([wk_ref[2 * part], wk_ref[2 * part + 1]], axis=1)
        start = part * PAYLOAD
        payload_ref[start : start + 8, :] = jnp.where(k < 5, first, pltpu.roll(wk, 5, 0))
        payload_ref[start + 8 : start + 16, :] = jnp.where(
            (k < 5) | (k == 7), second, pltpu.roll(wk, 2, 0)
        )
        payload_ref[start + 16 : start + 24, :] = third


def totals_of(payload_ref, scaled_ref):
    total = payload_ref[0:PAYLOAD, :]
    for part in range(1, PARTS):
        total = total + payload_ref[part * PAYLOAD : (part + 1) * PAYLOAD, :]
    first, second, third = total[0:8], total[8:16], total[16:24]
    k = iota((8, CELLS), 0)
    mine = k < 5
    wk = jnp.where(k < 3, pltpu.roll(first, 3, 0), jnp.where(mine, pltpu.roll(second, 6, 0), 0.0))
    down = jnp.where(k == 1, pltpu.roll(second, 2, 0), jnp.where(mine, pltpu.roll(third, 5, 0), 0.0))
    down = jnp.where(k == 0, second - COURANT_SCALE * pltpu.roll(first, 7, 0), down)
    first, second, small = [jnp.where(mine, g, 0.0) for g in (first, second, third)]
    inverse = inverse_of(small[:, 0:128])
    rows = scaled_ref[NODES : NODES + 8, :]
    coeffs = rows[1:2] * apply_small(inverse, 8, rows[2:3] * first)
    return (first, second, down), wk, small, inverse, coeffs


def middle_kernel(payload_ref, scaled_ref, copies_ref, block_ref, own_ref, sems, own_sems):
    group, wk, small, inverse, coeffs = totals_of(payload_ref, scaled_ref)
    z_speed = scaled_ref[NODES + 3 : NODES + 4, :]
    copies = []
    for i in range(PIECES):
        for m in range(i * Q // PIECES, (i + 1) * Q // PIECES):
            rows = slice(Q * m, Q * m + Q)
            s = scaled_ref[rows, :] + equilibrium_rows(m, coeffs, z_speed)
            block_ref[rows, :] = s.astype(BF16)
        copies += in_parts(NODES + EXTRA, 0, i, PIECES, block_ref, copies_ref, sems)
    pieces = jnp.concatenate([p.astype(F32) for p in split(wk, 3)], axis=0).astype(BF16)
    own = KERNEL_STEP * three_sum(jnp.dot(pieces, block_ref[...], preferred_element_type=F32))
    own = own - scaled_ref[NODES + 8 :, :]
    own_ref[...] = jnp.concatenate([p.astype(F32) for p in split(own, 2)], axis=0).astype(BF16)
    copies += in_parts(NODES + EXTRA, NODES, 0, 1, own_ref, copies_ref, own_sems)
    for copy in copies:
        copy.wait()


def state_kernel(payload_ref, scaled_ref, state_ref, low_ref, high_ref):
    group, wk, small, inverse, coeffs = totals_of(payload_ref, scaled_ref)
    z_speed = scaled_ref[NODES + 3 : NODES + 4, :]
    from_eq = [apply_small(small, 8 * t, coeffs) for t in range(GROUPS)]
    flux = from_eq[1] + from_eq[2]
    for t, shift in ((3, from_below_y), (4, from_above_y), (5, from_below_z), (6, from_above_z)):
        flux = flux + (from_eq[t] - shift(from_eq[t]))
    high_ref[NODES // 2 :, :] = group[1] + from_eq[1]
    low_ref[NODES // 2 :, :] = group[2] + from_eq[2]
    for m in range(Q):
        rows = slice(Q * m, Q * m + Q)
        s = scaled_ref[rows, :] + equilibrium_rows(m, coeffs, z_speed)
        state_ref[rows, :] = s
        store_sides(m, s, low_ref, high_ref)
    state_ref[NODES : NODES + 8, :] = group[0] + from_eq[0] - flux
    state_ref[NODES + 8 :, :] = jnp.concatenate([inverse, inverse], axis=1)


def second_base_kernel(z_ref, state_ref, rate_ref, above_ref, below_ref, base_ref):
    z_speed = z_ref[0]
    rate = rate_ref[...]
    keep = 1.0 / (1.0 + rate)
    for m in range(Q):
        rows = slice(Q * m, Q * m + Q)
        half = slice(8 * m, 8 * m + 8)
        e = advected_rows(m, state_ref[rows, :], below_ref[half, :], above_ref[half, :], z_speed)
        base_ref[rows, :] = keep * e
    sides_part = above_ref[NODES // 2 :, :] + below_ref[NODES // 2 :, :]
    base_ref[NODES : NODES + 8, :] = state_ref[NODES : NODES + 8, :] + sides_part
    base_ref[NODES + 8 : NODES + 16, :] = state_ref[NODES + 8 : NODES + 16, :]
    base_ref[NODES + 16 :, :] = step_rows(rate, z_speed)


def last_kernel(
    dense_ref, base_ref, gathered_ref, out_ref, term_ref, held_ref, own_ref, sems, own_sems
):
    stride = NODES + EXTRA
    copies = fetch(gathered_ref, stride, held_ref, sems)
    extra = []
    for part in range(PARTS):
        source = gathered_ref.at[part * stride + NODES : (part + 1) * stride]
        at = slice(part * EXTRA, (part + 1) * EXTRA)
        extra.append(pltpu.make_async_copy(source, own_ref.at[at], own_sems.at[part]))
        extra[-1].start()
    term_ref[...] = product(dense_ref, held_ref, copies)
    for copy in extra:
        copy.wait()
    total = base_ref[NODES : NODES + 8, :]
    for part in range(PARTS):
        own = own_ref[part * EXTRA : (part + 1) * EXTRA, :].astype(F32)
        total = total + (own[0:8] + own[8:16])
    rows = base_ref[NODES + 16 :, :]
    coeffs = rows[1:2] * apply_small(base_ref[NODES + 8 : NODES + 16, 0:128], 8, total)
    for m in range(Q):
        at = slice(Q * m, Q * m + Q)
        new = base_ref[at, :] + rows[0:1] * term_ref[at, :] + equilibrium_rows(m, coeffs, rows[3:4])
        for h in range(2):
            out_ref[pl.ds(2 * Q * m + h, Q, stride=2), :] = new[:, 128 * h : 128 * h + 128]


VMEM = pl.BlockSpec(memory_space=pltpu.VMEM)
SMEM = pl.BlockSpec(memory_space=pltpu.SMEM)
HBM = pl.BlockSpec(memory_space=pltpu.HBM)


def call(kernel, scalars, arrays, outs, scratch=(), in_hbm=False, from_hbm=()):
    make = pltpu.HBM if in_hbm else jax.ShapeDtypeStruct
    from_hbm = [pltpu.with_memory_space_constraint(a, pltpu.HBM) for a in from_hbm]
    return pl.pallas_call(
        kernel,
        out_shape=[make(shape, kind) for shape, kind in outs],
        in_specs=[SMEM] * len(scalars) + [VMEM] * len(arrays) + [HBM] * len(from_hbm),
        out_specs=[HBM if in_hbm else VMEM] * len(outs),
        scratch_shapes=list(scratch),
        compiler_params=pltpu.CompilerParams(vmem_limit_bytes=VMEM_BYTES),
    )(*scalars, *arrays, *from_hbm)


def sides(low, high):
    count = lax.axis_size("gx")
    up = [(i, (i + 1) % count) for i in range(count)]
    down = [(target, source) for source, target in up]
    return lax.ppermute(low, "gx", down), lax.ppermute(high, "gx", up)


def spread(copies):
    return lax.all_to_all(copies, "vert", 0, 0, tiled=True)


def per_device(distribution, relax_rate, node_weight, kernel_tiles, tile_cols):
    state = distribution.reshape(2 * NODES, CELLS // 2)
    weight = node_weight.reshape(1, NODES)
    z_speed = speed_of(lax.axis_index("vert")).reshape(1)
    half = NODES // 2
    block = pltpu.VMEM((NODES, CELLS), BF16)
    held = pltpu.VMEM((PARTS * NODES, CELLS), BF16)
    sems = pltpu.SemaphoreType.DMA((PARTS,))
    many = pltpu.SemaphoreType.DMA((PIECES, PARTS))
    one = pltpu.SemaphoreType.DMA((1, PARTS))
    (copies,) = call(
        copies_kernel, [], [], [((PARTS * NODES, CELLS), BF16)],
        [pltpu.VMEM((2 * NODES, CELLS // 2), F32), block, sems, many], True, [state],
    )
    gathered = spread(copies)
    low, high, dense, phi, wk = call(
        prepare_kernel, [tile_cols, z_speed], [state, weight, kernel_tiles],
        [
            ((half, CELLS), F32), ((half, CELLS), F32), ((NODES, PARTS * NODES), BF16),
            ((8 * GROUPS + 8, NODES), F32), ((2 * PARTS, 8, TILE), F32),
        ],
    )
    above, below = sides(low, high)
    (base,) = call(
        base_kernel, [z_speed], [state, relax_rate, above, below], [((NODES + 8, CELLS), F32)]
    )
    scaled, payload = call(
        first_kernel, [], [dense, base, phi, wk],
        [((NODES + 16, CELLS), F32), ((PARTS * PAYLOAD, CELLS), F32)], [held, sems], False, [gathered],
    )
    payload = spread(payload)
    (copies,) = call(
        middle_kernel, [], [payload, scaled], [((PARTS * (NODES + EXTRA), CELLS), BF16)],
        [block, pltpu.VMEM((EXTRA, CELLS), BF16), many, one], True,
    )
    gathered = spread(copies)
    state, low, high = call(
        state_kernel, [], [payload, scaled],
        [((NODES + 16, CELLS), F32), ((half + 8, CELLS), F32), ((half + 8, CELLS), F32)],
    )
    above, below = sides(low, high)
    (base,) = call(
        second_base_kernel, [z_speed], [state, relax_rate, above, below],
        [((NODES + 24, CELLS), F32)],
    )
    (out,) = call(
        last_kernel, [], [dense, base], [((2 * NODES, CELLS // 2), F32)],
        [
            pltpu.VMEM((NODES, CELLS), F32), held, pltpu.VMEM((PARTS * EXTRA, CELLS), BF16), sems, sems,
        ],
        False, [gathered],
    )
    return out.reshape(distribution.shape)


def solution(mesh):
    placed = (
        P("vert", "gx", None),
        P("gx", None),
        P("vert"),
        P("vert", None, None),
        P("vert", None),
    )
    return jax.shard_map(
        per_device, mesh=mesh, in_specs=placed, out_specs=P("vert", "gx", None), check_vma=False
    )
```

```python
import functools

import jax
import jax.numpy as jnp
from jax import lax
from jax.experimental import pallas as pl
from jax.experimental.pallas import tpu as pltpu
from jax.sharding import PartitionSpec as P

Q = 16
TILE = 128
NB = 12
NZ = 4
CELLS = 256
NODES = 256
PARTS = 16
COURANT_SCALE = 0.3
KERNEL_STEP = 0.5
MIDDLE = (Q - 1) / 2.0
EXTRA = 16
PAYLOAD = 24
PIECES = 2
GROUPS = 7
F32 = jnp.float32
BF16 = jnp.bfloat16
HIGHEST = lax.Precision.HIGHEST
VMEM_BYTES = 24 * 1024 * 1024


def iota(shape, dim):
    return lax.broadcasted_iota(jnp.int32, shape, dim)


def speed_of(index):
    return (index.astype(F32) - MIDDLE) / MIDDLE


def from_below_y(a):
    return pltpu.roll(a, NZ, 1)


def from_above_y(a):
    return pltpu.roll(a, CELLS - NZ, 1)


def from_below_z(a):
    first = iota(a.shape, 1) % NZ == 0
    return jnp.where(first, pltpu.roll(a, CELLS - (NZ - 1), 1), pltpu.roll(a, 1, 1))


def from_above_z(a):
    last = iota(a.shape, 1) % NZ == NZ - 1
    return jnp.where(last, pltpu.roll(a, NZ - 1, 1), pltpu.roll(a, CELLS - 1, 1))


def split(a, pieces):
    out = []
    for _ in range(pieces):
        out.append(a.astype(BF16))
        a = a - out[-1].astype(F32)
    return out


def three_sum(a):
    return a[0:8] + a[8:16] + a[16:24]


def node_rows(z_speed):
    node = iota((8, NODES), 1)
    k = iota((8, NODES), 0)
    x, y = speed_of(node % Q), speed_of(node // Q)
    z = jnp.full((8, NODES), z_speed)
    invariants = jnp.where(k == 0, 1.0, 0.0)
    for row, value in ((1, x), (2, y), (3, z), (4, x * x + y * y + z * z)):
        invariants = jnp.where(k == row, value, invariants)
    factors = [None]
    for speed in (x, y, z):
        factors.append(COURANT_SCALE * jnp.maximum(speed, 0.0))
        factors.append(COURANT_SCALE * jnp.maximum(-speed, 0.0))
    return invariants, factors


def advected_rows(m, s, below, above, z_speed):
    row = iota((Q, CELLS), 0)
    lane = iota((Q, CELLS), 1)
    x_courant = COURANT_SCALE * jnp.abs(speed_of(row))
    y_courant = COURANT_SCALE * abs((m - MIDDLE) / MIDDLE)
    z_courant = COURANT_SCALE * jnp.abs(z_speed)
    up = z_speed > 0
    edge = jnp.where(up, 0, NZ - 1)
    near = pltpu.roll(s, jnp.where(up, 1, CELLS - 1), 1)
    far = pltpu.roll(s, jnp.where(up, CELLS - (NZ - 1), NZ - 1), 1)
    z_side = jnp.where(lane % NZ == edge, far, near)
    y_side = from_below_y(s) if m >= Q // 2 else from_above_y(s)
    x_side = jnp.concatenate([above, below], axis=0)
    flux = x_courant * (s - x_side) + y_courant * (s - y_side) + z_courant * (s - z_side)
    return s - flux


def equilibrium_rows(m, coeffs, z_speed):
    y = (m - MIDDLE) / MIDDLE
    x = speed_of(iota((Q, CELLS), 0))
    common = coeffs[0:1] + y * coeffs[2:3] + z_speed * coeffs[3:4]
    common = common + (y * y + z_speed * z_speed) * coeffs[4:5]
    return common + x * coeffs[1:2] + (x * x) * coeffs[4:5]


def apply_small(matrix, first, rows):
    total = matrix[:, first : first + 1] * rows[0:1]
    for k in range(1, 5):
        total = total + matrix[:, first + k : first + k + 1] * rows[k : k + 1]
    return total


def inverse_of(gram):
    row, lane = iota((8, 128), 0), iota((8, 128), 1)
    work = jnp.where((row < 5) & (lane < 5), gram, 0.0)
    work = jnp.where((lane == row + 8) | ((lane == row) & (row >= 5)), 1.0, work)
    for i in range(5):
        pivot = work[i : i + 1, :] / work[i : i + 1, i : i + 1]
        work = jnp.where(row == i, pivot, work - work[:, i : i + 1] * pivot)
    return work


def load_state(ref, m):
    halves = [ref[pl.ds(2 * Q * m + h, Q, stride=2), :] for h in range(2)]
    return jnp.concatenate(halves, axis=1)


def store_sides(m, s, low_ref, high_ref):
    low_ref[8 * m : 8 * m + 8, :] = s[0:8]
    high_ref[8 * m : 8 * m + 8, :] = s[8:16]


def in_parts(rows_per_part, start, piece, pieces, block_ref, copies_ref, sems):
    count = block_ref.shape[0] // pieces
    copies = []
    for part in range(PARTS):
        at = part * rows_per_part + start + piece * count
        copies.append(
            pltpu.make_async_copy(
                block_ref.at[piece * count : (piece + 1) * count],
                copies_ref.at[at : at + count],
                sems.at[piece, part],
            )
        )
        copies[-1].start()
    return copies


def copies_kernel(state_ref, copies_ref, held_ref, block_ref, in_sems, sems):
    pieces = []
    for i in range(PIECES):
        at = pl.ds(i * 2 * NODES // PIECES, 2 * NODES // PIECES)
        pieces.append(pltpu.make_async_copy(state_ref.at[at], held_ref.at[at], in_sems.at[i]))
        pieces[-1].start()
    copies = []
    for i in range(PIECES):
        pieces[i].wait()
        for m in range(i * Q // PIECES, (i + 1) * Q // PIECES):
            block_ref[Q * m : Q * m + Q, :] = load_state(held_ref, m).astype(BF16)
        copies += in_parts(NODES, 0, i, PIECES, block_ref, copies_ref, sems)
    for copy in copies:
        copy.wait()


def prepare_kernel(
    cols_ref, z_ref, state_ref, weight_ref, tiles_ref,
    low_ref, high_ref, wk_ref, phi_out_ref, phi_ref, sem,
):
    for m in range(Q):
        store_sides(m, load_state(state_ref, m), low_ref, high_ref)
    invariants, factors = node_rows(z_ref[0])
    base = weight_ref[...] * invariants
    phi = jnp.concatenate([base] + [base * f for f in factors[1:]], axis=0)
    phi_ref[0 : 8 * GROUPS, :] = phi
    padded = jnp.concatenate([phi, jnp.zeros((TILE - 8 * GROUPS, NODES), F32)], axis=0)
    small = lax.dot_general(
        invariants, padded, (((1,), (1,)), ((), ())), precision=HIGHEST, preferred_element_type=F32
    )
    phi_ref[8 * GROUPS :, :] = jnp.concatenate([small, jnp.zeros((8, CELLS - TILE), F32)], axis=1)
    copy = pltpu.make_async_copy(phi_ref, phi_out_ref, sem)
    copy.start()
    wk_ref[...] = jnp.zeros_like(wk_ref)
    pieces = jnp.concatenate([p.astype(F32) for p in split(base, 3)], axis=0).astype(BF16)
    for r in range(2):
        part = three_sum(
            jnp.dot(pieces[:, r * TILE : (r + 1) * TILE], tiles_ref[r], preferred_element_type=F32)
        )
        for j in range(NB):
            at = slice(j * TILE, (j + 1) * TILE)
            col = cols_ref[r, j]
            wk_ref[col] = wk_ref[col] + part[:, at]
    copy.wait()


def step_rows(rate, z_speed):
    keep = 1.0 / (1.0 + rate)
    rows = [KERNEL_STEP * keep, rate * keep, 1.0 + rate, jnp.full((1, CELLS), z_speed)]
    return jnp.concatenate(rows + [jnp.zeros((4, CELLS), F32)], axis=0)


def base_kernel(z_ref, state_ref, rate_ref, above_ref, below_ref, base_ref):
    z_speed = z_ref[0]
    rate = rate_ref[...]
    keep = 1.0 / (1.0 + rate)
    for m in range(Q):
        half = slice(8 * m, 8 * m + 8)
        s = load_state(state_ref, m)
        e = advected_rows(m, s, below_ref[half, :], above_ref[half, :], z_speed)
        base_ref[Q * m : Q * m + Q, :] = keep * e
    base_ref[NODES:, :] = step_rows(rate, z_speed)


def kernel_product(cols_ref, tiles_ref, gathered_ref, stride, term_ref):
    for r in range(2):
        blocks = []
        for j in range(NB):
            col = cols_ref[r, j]
            start = (col // 2) * stride + (col % 2) * TILE
            blocks.append(gathered_ref[pl.ds(pl.multiple_of(start, 16), TILE), :])
        term_ref[r * TILE : (r + 1) * TILE, :] = jnp.dot(
            tiles_ref[r], jnp.concatenate(blocks, axis=0), preferred_element_type=F32
        )


def first_kernel(
    cols_ref, tiles_ref, gathered_ref, base_ref, wk_ref, phi_in_ref,
    scaled_ref, payload_ref, term_ref, phi_ref, sem,
):
    copy = pltpu.make_async_copy(phi_in_ref, phi_ref, sem)
    copy.start()
    kernel_product(cols_ref, tiles_ref, gathered_ref, NODES, term_ref)
    scaled = base_ref[0:NODES, :] + base_ref[NODES : NODES + 1, :] * term_ref[...]
    scaled_ref[0:NODES, :] = scaled
    scaled_ref[NODES : NODES + 8, :] = base_ref[NODES:, :]
    copy.wait()
    phi = phi_ref[0 : 8 * GROUPS, :]
    moments = jnp.dot(phi, scaled, precision=HIGHEST, preferred_element_type=F32)
    group = [moments[8 * t : 8 * t + 8] for t in range(GROUPS)]
    flux = group[1] + group[2]
    for t, shift in ((3, from_below_y), (4, from_above_y), (5, from_below_z), (6, from_above_z)):
        flux = flux + (group[t] - shift(group[t]))
    scaled_ref[NODES + 8 :, :] = flux
    k = iota((8, CELLS), 0)
    first = group[0]
    second = jnp.where(k < 5, group[1], pltpu.roll(group[2], 6, 0))
    third = jnp.where(k < 5, phi_ref[8 * GROUPS :, :], pltpu.roll(group[2], 3, 0))
    for part in range(PARTS):
        wk = jnp.concatenate([wk_ref[2 * part], wk_ref[2 * part + 1]], axis=1)
        start = part * PAYLOAD
        payload_ref[start : start + 8, :] = jnp.where(k < 5, first, pltpu.roll(wk, 5, 0))
        payload_ref[start + 8 : start + 16, :] = jnp.where(
            (k < 5) | (k == 7), second, pltpu.roll(wk, 2, 0)
        )
        payload_ref[start + 16 : start + 24, :] = third


def totals_of(payload_ref, scaled_ref):
    total = payload_ref[0:PAYLOAD, :]
    for part in range(1, PARTS):
        total = total + payload_ref[part * PAYLOAD : (part + 1) * PAYLOAD, :]
    first, second, third = total[0:8], total[8:16], total[16:24]
    k = iota((8, CELLS), 0)
    mine = k < 5
    wk = jnp.where(k < 3, pltpu.roll(first, 3, 0), jnp.where(mine, pltpu.roll(second, 6, 0), 0.0))
    down = jnp.where(k == 1, pltpu.roll(second, 2, 0), jnp.where(mine, pltpu.roll(third, 5, 0), 0.0))
    down = jnp.where(k == 0, second - COURANT_SCALE * pltpu.roll(first, 7, 0), down)
    first, second, small = [jnp.where(mine, g, 0.0) for g in (first, second, third)]
    inverse = inverse_of(small[:, 0:128])
    rows = scaled_ref[NODES : NODES + 8, :]
    coeffs = rows[1:2] * apply_small(inverse, 8, rows[2:3] * first)
    return (first, second, down), wk, small, inverse, coeffs


def middle_kernel(payload_ref, scaled_ref, copies_ref, block_ref, own_ref, sems, own_sems):
    group, wk, small, inverse, coeffs = totals_of(payload_ref, scaled_ref)
    z_speed = scaled_ref[NODES + 3 : NODES + 4, :]
    copies = []
    for i in range(PIECES):
        for m in range(i * Q // PIECES, (i + 1) * Q // PIECES):
            rows = slice(Q * m, Q * m + Q)
            s = scaled_ref[rows, :] + equilibrium_rows(m, coeffs, z_speed)
            block_ref[rows, :] = s.astype(BF16)
        copies += in_parts(NODES + EXTRA, 0, i, PIECES, block_ref, copies_ref, sems)
    pieces = jnp.concatenate([p.astype(F32) for p in split(wk, 3)], axis=0).astype(BF16)
    own = KERNEL_STEP * three_sum(jnp.dot(pieces, block_ref[...], preferred_element_type=F32))
    own = own - scaled_ref[NODES + 8 :, :]
    own_ref[...] = jnp.concatenate([p.astype(F32) for p in split(own, 2)], axis=0).astype(BF16)
    copies += in_parts(NODES + EXTRA, NODES, 0, 1, own_ref, copies_ref, own_sems)
    for copy in copies:
        copy.wait()


def state_kernel(payload_ref, scaled_ref, state_ref, low_ref, high_ref):
    group, wk, small, inverse, coeffs = totals_of(payload_ref, scaled_ref)
    z_speed = scaled_ref[NODES + 3 : NODES + 4, :]
    from_eq = [apply_small(small, 8 * t, coeffs) for t in range(GROUPS)]
    flux = from_eq[1] + from_eq[2]
    for t, shift in ((3, from_below_y), (4, from_above_y), (5, from_below_z), (6, from_above_z)):
        flux = flux + (from_eq[t] - shift(from_eq[t]))
    high_ref[NODES // 2 :, :] = group[1] + from_eq[1]
    low_ref[NODES // 2 :, :] = group[2] + from_eq[2]
    for m in range(Q):
        rows = slice(Q * m, Q * m + Q)
        s = scaled_ref[rows, :] + equilibrium_rows(m, coeffs, z_speed)
        state_ref[rows, :] = s
        store_sides(m, s, low_ref, high_ref)
    state_ref[NODES : NODES + 8, :] = group[0] + from_eq[0] - flux
    state_ref[NODES + 8 :, :] = jnp.concatenate([inverse, inverse], axis=1)


def second_base_kernel(z_ref, state_ref, rate_ref, above_ref, below_ref, base_ref):
    z_speed = z_ref[0]
    rate = rate_ref[...]
    keep = 1.0 / (1.0 + rate)
    for m in range(Q):
        rows = slice(Q * m, Q * m + Q)
        half = slice(8 * m, 8 * m + 8)
        e = advected_rows(m, state_ref[rows, :], below_ref[half, :], above_ref[half, :], z_speed)
        base_ref[rows, :] = keep * e
    sides_part = above_ref[NODES // 2 :, :] + below_ref[NODES // 2 :, :]
    base_ref[NODES : NODES + 8, :] = state_ref[NODES : NODES + 8, :] + sides_part
    base_ref[NODES + 8 : NODES + 16, :] = state_ref[NODES + 8 : NODES + 16, :]
    base_ref[NODES + 16 :, :] = step_rows(rate, z_speed)


def last_kernel(cols_ref, tiles_ref, gathered_ref, base_ref, out_ref, term_ref):
    stride = NODES + EXTRA
    kernel_product(cols_ref, tiles_ref, gathered_ref, stride, term_ref)
    total = base_ref[NODES : NODES + 8, :]
    for part in range(PARTS):
        own = gathered_ref[part * stride + NODES : (part + 1) * stride, :].astype(F32)
        total = total + (own[0:8] + own[8:16])
    rows = base_ref[NODES + 16 :, :]
    coeffs = rows[1:2] * apply_small(base_ref[NODES + 8 : NODES + 16, 0:128], 8, total)
    for m in range(Q):
        at = slice(Q * m, Q * m + Q)
        new = base_ref[at, :] + rows[0:1] * term_ref[at, :] + equilibrium_rows(m, coeffs, rows[3:4])
        for h in range(2):
            out_ref[pl.ds(2 * Q * m + h, Q, stride=2), :] = new[:, 128 * h : 128 * h + 128]


VMEM = pl.BlockSpec(memory_space=pltpu.VMEM)
SMEM = pl.BlockSpec(memory_space=pltpu.SMEM)
HBM = pl.BlockSpec(memory_space=pltpu.HBM)


def call(kernel, scalars, arrays, outs, scratch=(), in_hbm=(), from_hbm=()):
    from_hbm = [pltpu.with_memory_space_constraint(a, pltpu.HBM) for a in from_hbm]
    return pl.pallas_call(
        kernel,
        out_shape=[
            (pltpu.HBM if i in in_hbm else jax.ShapeDtypeStruct)(shape, kind) for i, (shape, kind) in enumerate(outs)
        ],
        in_specs=[SMEM] * len(scalars) + [VMEM] * len(arrays) + [HBM] * len(from_hbm),
        out_specs=[HBM if i in in_hbm else VMEM for i in range(len(outs))],
        scratch_shapes=list(scratch),
        compiler_params=pltpu.CompilerParams(vmem_limit_bytes=VMEM_BYTES),
    )(*scalars, *arrays, *from_hbm)


def sides(low, high):
    count = lax.axis_size("gx")
    up = [(i, (i + 1) % count) for i in range(count)]
    down = [(target, source) for source, target in up]
    return lax.ppermute(low, "gx", down), lax.ppermute(high, "gx", up)


def spread(copies):
    return lax.all_to_all(copies, "vert", 0, 0, tiled=True)


def per_device(distribution, relax_rate, node_weight, kernel_tiles, tile_cols):
    state = distribution.reshape(2 * NODES, CELLS // 2)
    weight = node_weight.reshape(1, NODES)
    z_speed = speed_of(lax.axis_index("vert")).reshape(1)
    half = NODES // 2
    block = pltpu.VMEM((NODES, CELLS), BF16)
    term = pltpu.VMEM((NODES, CELLS), F32)
    sems = pltpu.SemaphoreType.DMA((PARTS,))
    phi_rows = pltpu.VMEM((8 * GROUPS + 8, NODES), F32)
    dma = pltpu.SemaphoreType.DMA
    many = pltpu.SemaphoreType.DMA((PIECES, PARTS))
    one = pltpu.SemaphoreType.DMA((1, PARTS))
    (copies,) = call(
        copies_kernel, [], [], [((PARTS * NODES, CELLS), BF16)],
        [pltpu.VMEM((2 * NODES, CELLS // 2), F32), block, sems, many], (0,), [state],
    )
    gathered = spread(copies)
    low, high, wk, phi = call(
        prepare_kernel, [tile_cols, z_speed], [state, weight, kernel_tiles],
        [
            ((half, CELLS), F32), ((half, CELLS), F32), ((2 * PARTS, 8, TILE), F32),
            ((8 * GROUPS + 8, NODES), F32),
        ],
        [phi_rows, dma], (3,),
    )
    above, below = sides(low, high)
    (base,) = call(
        base_kernel, [z_speed], [state, relax_rate, above, below], [((NODES + 8, CELLS), F32)]
    )
    scaled, payload = call(
        first_kernel, [tile_cols], [kernel_tiles, gathered, base, wk],
        [((NODES + 16, CELLS), F32), ((PARTS * PAYLOAD, CELLS), F32)], [term, phi_rows, dma], (), [phi],
    )
    payload = spread(payload)
    (copies,) = call(
        middle_kernel, [], [payload, scaled], [((PARTS * (NODES + EXTRA), CELLS), BF16)],
        [block, pltpu.VMEM((EXTRA, CELLS), BF16), many, one], (0,),
    )
    gathered = spread(copies)
    state, low, high = call(
        state_kernel, [], [payload, scaled],
        [((NODES + 16, CELLS), F32), ((half + 8, CELLS), F32), ((half + 8, CELLS), F32)],
    )
    above, below = sides(low, high)
    (base,) = call(
        second_base_kernel, [z_speed], [state, relax_rate, above, below],
        [((NODES + 24, CELLS), F32)],
    )
    (out,) = call(
        last_kernel, [tile_cols], [kernel_tiles, gathered, base],
        [((2 * NODES, CELLS // 2), F32)], [term],
    )
    return out.reshape(distribution.shape)


def solution(mesh):
    placed = (
        P("vert", "gx", None),
        P("gx", None),
        P("vert"),
        P("vert", None, None),
        P("vert", None),
    )
    return jax.shard_map(
        per_device, mesh=mesh, in_specs=placed, out_specs=P("vert", "gx", None), check_vma=False
    )
```

```python
import functools

import jax
import jax.numpy as jnp
from jax import lax
from jax.experimental import pallas as pl
from jax.experimental.pallas import tpu as pltpu
from jax.sharding import PartitionSpec as P

Q = 16
TILE = 128
NB = 12
NZ = 4
CELLS = 256
NODES = 256
PARTS = 16
COURANT_SCALE = 0.3
KERNEL_STEP = 0.5
MIDDLE = (Q - 1) / 2.0
EXTRA = 16
PAYLOAD = 24
SIDE = 4
GROUPS = 7
F32 = jnp.float32
BF16 = jnp.bfloat16
HIGHEST = lax.Precision.HIGHEST
VMEM_BYTES = 24 * 1024 * 1024


def iota(shape, dim):
    return lax.broadcasted_iota(jnp.int32, shape, dim)


def speed_of(index):
    return (index.astype(F32) - MIDDLE) / MIDDLE


def from_below_y(a):
    return pltpu.roll(a, NZ, 1)


def from_above_y(a):
    return pltpu.roll(a, CELLS - NZ, 1)


def from_below_z(a):
    first = iota(a.shape, 1) % NZ == 0
    return jnp.where(first, pltpu.roll(a, CELLS - (NZ - 1), 1), pltpu.roll(a, 1, 1))


def from_above_z(a):
    last = iota(a.shape, 1) % NZ == NZ - 1
    return jnp.where(last, pltpu.roll(a, NZ - 1, 1), pltpu.roll(a, CELLS - 1, 1))


def split(a, pieces):
    out = []
    for _ in range(pieces):
        out.append(a.astype(BF16))
        a = a - out[-1].astype(F32)
    return out


def three_sum(a):
    return a[0:8] + a[8:16] + a[16:24]


def node_rows(z_speed):
    node = iota((8, NODES), 1)
    k = iota((8, NODES), 0)
    x, y = speed_of(node % Q), speed_of(node // Q)
    z = jnp.broadcast_to(z_speed, (8, NODES))
    invariants = jnp.where(k == 0, 1.0, 0.0)
    for row, value in ((1, x), (2, y), (3, z), (4, x * x + y * y + z * z)):
        invariants = jnp.where(k == row, value, invariants)
    factors = [None]
    for speed in (x, y, z):
        factors.append(COURANT_SCALE * jnp.maximum(speed, 0.0))
        factors.append(COURANT_SCALE * jnp.maximum(-speed, 0.0))
    return invariants, factors


def weights_rows(z_speed, weight):
    invariants, factors = node_rows(z_speed)
    base = weight * invariants
    return invariants, base, jnp.concatenate([base] + [base * f for f in factors[1:]], axis=0)


def advected_rows(m, s, below, above, z_speed):
    row = iota((Q, CELLS), 0)
    lane = iota((Q, CELLS), 1)
    x_courant = COURANT_SCALE * jnp.abs(speed_of(row))
    y_courant = COURANT_SCALE * abs((m - MIDDLE) / MIDDLE)
    z_courant = COURANT_SCALE * jnp.abs(z_speed)
    up = z_speed > 0
    edge = jnp.where(up, 0, NZ - 1)
    near = pltpu.roll(s, jnp.where(up, 1, CELLS - 1), 1)
    far = pltpu.roll(s, jnp.where(up, CELLS - (NZ - 1), NZ - 1), 1)
    z_side = jnp.where(lane % NZ == edge, far, near)
    y_side = from_below_y(s) if m >= Q // 2 else from_above_y(s)
    x_side = jnp.concatenate([above, below], axis=0)
    flux = x_courant * (s - x_side) + y_courant * (s - y_side) + z_courant * (s - z_side)
    return s - flux


def equilibrium_rows(m, coeffs, z_speed):
    y = (m - MIDDLE) / MIDDLE
    x = speed_of(iota((Q, CELLS), 0))
    common = coeffs[0:1] + y * coeffs[2:3] + z_speed * coeffs[3:4]
    common = common + (y * y + z_speed * z_speed) * coeffs[4:5]
    return common + x * coeffs[1:2] + (x * x) * coeffs[4:5]


def apply_small(matrix, first, rows):
    total = matrix[:, first : first + 1] * rows[0:1]
    for k in range(1, 5):
        total = total + matrix[:, first + k : first + k + 1] * rows[k : k + 1]
    return total


def inverse_of(gram):
    row, lane = iota((8, 128), 0), iota((8, 128), 1)
    work = jnp.where((row < 5) & (lane < 5), gram, 0.0)
    work = jnp.where((lane == row + 8) | ((lane == row) & (row >= 5)), 1.0, work)
    for i in range(5):
        pivot = work[i : i + 1, :] / work[i : i + 1, i : i + 1]
        work = jnp.where(row == i, pivot, work - work[:, i : i + 1] * pivot)
    return work


def load_state(ref, m):
    halves = [ref[pl.ds(2 * Q * m + h, Q, stride=2), :] for h in range(2)]
    return jnp.concatenate(halves, axis=1)


def store_sides(m, s, low_ref, high_ref):
    low_ref[8 * m : 8 * m + 8, :] = s[0:8]
    high_ref[8 * m : 8 * m + 8, :] = s[8:16]


def copies_kernel(state_ref, copies_ref):
    for m in range(Q):
        rounded = load_state(state_ref, m).astype(BF16)
        for part in range(SIDE):
            copies_ref[part * NODES + Q * m : part * NODES + Q * m + Q, :] = rounded


def arrival(place_ref, col):
    first, y, x = place_ref[0], place_ref[1], place_ref[2]
    from_y, from_x = col // (2 * SIDE), col // 2 % SIDE
    bundle = jnp.where(first == 0, y - from_y, x - from_x)
    bundle = jnp.where(bundle < 0, bundle + SIDE, bundle)
    return (bundle * SIDE + jnp.where(first == 0, from_x, from_y)) * 2 + col % 2


def prepare_kernel(
    cols_ref, place_ref, z_ref, state_ref, weight_ref, tiles_ref,
    low_ref, high_ref, dense_ref, wk_out_ref, wk_ref, sem,
):
    for m in range(Q):
        store_sides(m, load_state(state_ref, m), low_ref, high_ref)
    invariants, base, phi = weights_rows(z_ref[0], weight_ref[...])
    padded = jnp.concatenate([phi, jnp.zeros((TILE - 8 * GROUPS, NODES), F32)], axis=0)
    small = lax.dot_general(
        invariants, padded, (((1,), (1,)), ((), ())), precision=HIGHEST, preferred_element_type=F32
    )
    wk_ref[...] = jnp.zeros_like(wk_ref)
    dense_ref[...] = jnp.zeros_like(dense_ref)
    wk_ref[2 * PARTS] = small
    pieces = jnp.concatenate([p.astype(F32) for p in split(base, 3)], axis=0).astype(BF16)
    for r in range(2):
        part = three_sum(
            jnp.dot(pieces[:, r * TILE : (r + 1) * TILE], tiles_ref[r], preferred_element_type=F32)
        )
        for j in range(NB):
            at = slice(j * TILE, (j + 1) * TILE)
            col = cols_ref[r, j]
            wk_ref[col] = wk_ref[col] + part[:, at]
            where = pl.ds(pl.multiple_of(arrival(place_ref, col) * TILE, TILE), TILE)
            dense_ref[r * TILE : (r + 1) * TILE, where] = tiles_ref[r, :, at]
    copy = pltpu.make_async_copy(wk_ref, wk_out_ref, sem)
    copy.start()
    copy.wait()


def step_rows(rate, z_speed):
    keep = 1.0 / (1.0 + rate)
    rows = [KERNEL_STEP * keep, rate * keep, 1.0 + rate, jnp.full((1, CELLS), z_speed)]
    return jnp.concatenate(rows + [jnp.zeros((4, CELLS), F32)], axis=0)


def base_kernel(z_ref, state_ref, rate_ref, weight_ref, above_ref, below_ref, base_ref):
    z_speed = z_ref[0]
    rate = rate_ref[...]
    keep = 1.0 / (1.0 + rate)
    for m in range(Q):
        half = slice(8 * m, 8 * m + 8)
        s = load_state(state_ref, m)
        e = advected_rows(m, s, below_ref[half, :], above_ref[half, :], z_speed)
        base_ref[Q * m : Q * m + Q, :] = keep * e
    base_ref[NODES:, :] = step_rows(rate, z_speed)
    base_ref[NODES + 4 : NODES + 5, :] = weight_ref[...]


def kernel_product(dense_ref, bundle_refs, stride):
    total = None
    for i, ref in enumerate(bundle_refs):
        blocks = [ref[j * stride : j * stride + NODES, :] for j in range(SIDE)]
        at = slice(i * SIDE * NODES, (i + 1) * SIDE * NODES)
        part = jnp.dot(
            dense_ref[:, at], jnp.concatenate(blocks, axis=0), preferred_element_type=F32
        )
        total = part if total is None else total + part
    return total


def first_kernel(
    dense_ref, base_ref, own_ref, near_ref, far_ref, back_ref, wk_in_ref,
    scaled_ref, payload_ref, wk_ref, sem,
):
    copy = pltpu.make_async_copy(wk_in_ref, wk_ref, sem)
    copy.start()
    term = kernel_product(dense_ref, (own_ref, near_ref, far_ref, back_ref), NODES)
    scaled = base_ref[0:NODES, :] + base_ref[NODES : NODES + 1, :] * term
    scaled_ref[0:NODES, :] = scaled
    scaled_ref[NODES : NODES + 8, :] = base_ref[NODES:, :]
    rows = base_ref[NODES:, :]
    _, _, phi = weights_rows(rows[3:4], rows[4:5])
    moments = jnp.dot(phi, scaled, precision=HIGHEST, preferred_element_type=F32)
    group = [moments[8 * t : 8 * t + 8] for t in range(GROUPS)]
    flux = group[1] + group[2]
    for t, shift in ((3, from_below_y), (4, from_above_y), (5, from_below_z), (6, from_above_z)):
        flux = flux + (group[t] - shift(group[t]))
    scaled_ref[NODES + 8 :, :] = flux
    k = iota((8, CELLS), 0)
    first = group[0]
    second = jnp.where(k < 5, group[1], pltpu.roll(group[2], 6, 0))
    copy.wait()
    small = jnp.concatenate([wk_ref[2 * PARTS], jnp.zeros((8, CELLS - TILE), F32)], axis=1)
    third = jnp.where(k < 5, small, pltpu.roll(group[2], 3, 0))
    for part in range(PARTS):
        wk = jnp.concatenate([wk_ref[2 * part], wk_ref[2 * part + 1]], axis=1)
        start = part * PAYLOAD
        payload_ref[start : start + 8, :] = jnp.where(k < 5, first, pltpu.roll(wk, 5, 0))
        payload_ref[start + 8 : start + 16, :] = jnp.where(
            (k < 5) | (k == 7), second, pltpu.roll(wk, 2, 0)
        )
        payload_ref[start + 16 : start + 24, :] = third


def totals_of(payload_ref, scaled_ref):
    total = payload_ref[0:PAYLOAD, :]
    for part in range(1, PARTS):
        total = total + payload_ref[part * PAYLOAD : (part + 1) * PAYLOAD, :]
    first, second, third = total[0:8], total[8:16], total[16:24]
    k = iota((8, CELLS), 0)
    mine = k < 5
    wk = jnp.where(k < 3, pltpu.roll(first, 3, 0), jnp.where(mine, pltpu.roll(second, 6, 0), 0.0))
    down = jnp.where(k == 1, pltpu.roll(second, 2, 0), jnp.where(mine, pltpu.roll(third, 5, 0), 0.0))
    down = jnp.where(k == 0, second - COURANT_SCALE * pltpu.roll(first, 7, 0), down)
    first, second, small = [jnp.where(mine, g, 0.0) for g in (first, second, third)]
    inverse = inverse_of(small[:, 0:128])
    rows = scaled_ref[NODES : NODES + 8, :]
    coeffs = rows[1:2] * apply_small(inverse, 8, rows[2:3] * first)
    return (first, second, down), wk, small, inverse, coeffs


def middle_kernel(payload_ref, scaled_ref, copies_ref, block_ref):
    group, wk, small, inverse, coeffs = totals_of(payload_ref, scaled_ref)
    z_speed = scaled_ref[NODES + 3 : NODES + 4, :]
    for m in range(Q):
        rows = slice(Q * m, Q * m + Q)
        s = scaled_ref[rows, :] + equilibrium_rows(m, coeffs, z_speed)
        rounded = s.astype(BF16)
        block_ref[rows, :] = rounded
        for part in range(SIDE):
            start = part * (NODES + EXTRA) + Q * m
            copies_ref[start : start + Q, :] = rounded
    pieces = jnp.concatenate([p.astype(F32) for p in split(wk, 3)], axis=0).astype(BF16)
    own = KERNEL_STEP * three_sum(jnp.dot(pieces, block_ref[...], preferred_element_type=F32))
    own = own - scaled_ref[NODES + 8 :, :]
    own = jnp.concatenate([p.astype(F32) for p in split(own, 2)], axis=0).astype(BF16)
    for part in range(SIDE):
        start = part * (NODES + EXTRA) + NODES
        copies_ref[start : start + EXTRA, :] = own


def state_kernel(payload_ref, scaled_ref, state_ref, low_ref, high_ref):
    group, wk, small, inverse, coeffs = totals_of(payload_ref, scaled_ref)
    z_speed = scaled_ref[NODES + 3 : NODES + 4, :]
    from_eq = [apply_small(small, 8 * t, coeffs) for t in range(GROUPS)]
    flux = from_eq[1] + from_eq[2]
    for t, shift in ((3, from_below_y), (4, from_above_y), (5, from_below_z), (6, from_above_z)):
        flux = flux + (from_eq[t] - shift(from_eq[t]))
    high_ref[NODES // 2 :, :] = group[1] + from_eq[1]
    low_ref[NODES // 2 :, :] = group[2] + from_eq[2]
    for m in range(Q):
        rows = slice(Q * m, Q * m + Q)
        s = scaled_ref[rows, :] + equilibrium_rows(m, coeffs, z_speed)
        state_ref[rows, :] = s
        store_sides(m, s, low_ref, high_ref)
    state_ref[NODES : NODES + 8, :] = group[0] + from_eq[0] - flux
    state_ref[NODES + 8 :, :] = jnp.concatenate([inverse, inverse], axis=1)


def second_base_kernel(z_ref, state_ref, rate_ref, above_ref, below_ref, base_ref):
    z_speed = z_ref[0]
    rate = rate_ref[...]
    keep = 1.0 / (1.0 + rate)
    for m in range(Q):
        rows = slice(Q * m, Q * m + Q)
        half = slice(8 * m, 8 * m + 8)
        e = advected_rows(m, state_ref[rows, :], below_ref[half, :], above_ref[half, :], z_speed)
        base_ref[rows, :] = keep * e
    sides_part = above_ref[NODES // 2 :, :] + below_ref[NODES // 2 :, :]
    base_ref[NODES : NODES + 8, :] = state_ref[NODES : NODES + 8, :] + sides_part
    base_ref[NODES + 8 : NODES + 16, :] = state_ref[NODES + 8 : NODES + 16, :]
    base_ref[NODES + 16 :, :] = step_rows(rate, z_speed)


def last_kernel(dense_ref, base_ref, own_ref, near_ref, far_ref, back_ref, out_ref, term_ref):
    stride = NODES + EXTRA
    bundles = (own_ref, near_ref, far_ref, back_ref)
    term_ref[...] = kernel_product(dense_ref, bundles, stride)
    total = base_ref[NODES : NODES + 8, :]
    for ref in bundles:
        for j in range(SIDE):
            own = ref[j * stride + NODES : (j + 1) * stride, :].astype(F32)
            total = total + (own[0:8] + own[8:16])
    rows = base_ref[NODES + 16 :, :]
    coeffs = rows[1:2] * apply_small(base_ref[NODES + 8 : NODES + 16, 0:128], 8, total)
    for m in range(Q):
        at = slice(Q * m, Q * m + Q)
        new = base_ref[at, :] + rows[0:1] * term_ref[at, :] + equilibrium_rows(m, coeffs, rows[3:4])
        for h in range(2):
            out_ref[pl.ds(2 * Q * m + h, Q, stride=2), :] = new[:, 128 * h : 128 * h + 128]


VMEM = pl.BlockSpec(memory_space=pltpu.VMEM)
SMEM = pl.BlockSpec(memory_space=pltpu.SMEM)
HBM = pl.BlockSpec(memory_space=pltpu.HBM)


def call(kernel, scalars, arrays, outs, scratch=(), in_hbm=(), from_hbm=()):
    from_hbm = [pltpu.with_memory_space_constraint(a, pltpu.HBM) for a in from_hbm]
    return pl.pallas_call(
        kernel,
        out_shape=[
            (pltpu.HBM if i in in_hbm else jax.ShapeDtypeStruct)(shape, kind) for i, (shape, kind) in enumerate(outs)
        ],
        in_specs=[SMEM] * len(scalars) + [VMEM] * len(arrays) + [HBM] * len(from_hbm),
        out_specs=[HBM if i in in_hbm else VMEM for i in range(len(outs))],
        scratch_shapes=list(scratch),
        compiler_params=pltpu.CompilerParams(vmem_limit_bytes=VMEM_BYTES),
    )(*scalars, *arrays, *from_hbm)


def sides(low, high):
    count = lax.axis_size("gx")
    up = [(i, (i + 1) % count) for i in range(count)]
    down = [(target, source) for source, target in up]
    return lax.ppermute(low, "gx", down), lax.ppermute(high, "gx", up)


def spread(copies):
    return lax.all_to_all(copies, "vert", 0, 0, tiled=True)


def gather(copies):
    slabs = lax.axis_size("gx")
    groups, pairs = [], [[], [], []]
    for g in range(slabs):
        for i in range(SIDE):
            line = [i * SIDE + j if g % 2 == 0 else j * SIDE + i for j in range(SIDE)]
            groups.append([g * PARTS + v for v in line])
            for j in range(SIDE):
                for shift in (1, 2, 3):
                    y, x = (i + shift) % SIDE, j
                    ends = (i * SIDE + j, y * SIDE + x) if g % 2 == 0 else (j * SIDE + i, x * SIDE + y)
                    pairs[shift - 1].append(tuple(g * PARTS + v for v in ends))
    axes = ("gx", "vert")
    bundle = lax.all_to_all(copies, axes, 0, 0, axis_index_groups=groups, tiled=True)
    return [bundle] + [lax.ppermute(bundle, axes, p) for p in pairs]


def per_device(distribution, relax_rate, node_weight, kernel_tiles, tile_cols):
    state = distribution.reshape(2 * NODES, CELLS // 2)
    weight = node_weight.reshape(1, NODES)
    z_speed = speed_of(lax.axis_index("vert")).reshape(1)
    half = NODES // 2
    vert = lax.axis_index("vert")
    place = jnp.stack([lax.axis_index("gx") % 2, vert // SIDE, vert % SIDE]).astype(jnp.int32)
    wk_rows = (2 * PARTS + 1, 8, TILE)
    dma = pltpu.SemaphoreType.DMA
    (copies,) = call(copies_kernel, [], [state], [((SIDE * NODES, CELLS), BF16)])
    bundles = gather(copies)
    low, high, dense, wk = call(
        prepare_kernel, [tile_cols, place, z_speed], [state, weight, kernel_tiles],
        [
            ((half, CELLS), F32), ((half, CELLS), F32), ((NODES, PARTS * NODES), BF16), (wk_rows, F32),
        ],
        [pltpu.VMEM(wk_rows, F32), dma], (3,),
    )
    above, below = sides(low, high)
    (base,) = call(
        base_kernel, [z_speed], [state, relax_rate, weight, above, below], [((NODES + 8, CELLS), F32)]
    )
    scaled, payload = call(
        first_kernel, [], [dense, base, *bundles],
        [((NODES + 16, CELLS), F32), ((PARTS * PAYLOAD, CELLS), F32)],
        [pltpu.VMEM(wk_rows, F32), dma], (), [wk],
    )
    payload = spread(payload)
    (copies,) = call(
        middle_kernel, [], [payload, scaled], [((SIDE * (NODES + EXTRA), CELLS), BF16)],
        [pltpu.VMEM((NODES, CELLS), BF16)],
    )
    bundles = gather(copies)
    state, low, high = call(
        state_kernel, [], [payload, scaled],
        [((NODES + 16, CELLS), F32), ((half + 8, CELLS), F32), ((half + 8, CELLS), F32)],
    )
    above, below = sides(low, high)
    (base,) = call(
        second_base_kernel, [z_speed], [state, relax_rate, above, below],
        [((NODES + 24, CELLS), F32)],
    )
    (out,) = call(
        last_kernel, [], [dense, base, *bundles], [((2 * NODES, CELLS // 2), F32)],
        [pltpu.VMEM((NODES, CELLS), F32)],
    )
    return out.reshape(distribution.shape)


def solution(mesh):
    placed = (
        P("vert", "gx", None),
        P("gx", None),
        P("vert"),
        P("vert", None, None),
        P("vert", None),
    )
    return jax.shard_map(
        per_device, mesh=mesh, in_specs=placed, out_specs=P("vert", "gx", None), check_vma=False
    )
```

```python
import functools

import jax
import jax.numpy as jnp
from jax import lax
from jax.experimental import pallas as pl
from jax.experimental.pallas import tpu as pltpu
from jax.sharding import PartitionSpec as P

Q = 16
TILE = 128
NB = 12
NZ = 4
CELLS = 256
NODES = 256
PARTS = 16
COURANT_SCALE = 0.3
KERNEL_STEP = 0.5
MIDDLE = (Q - 1) / 2.0
EXTRA = 16
PAYLOAD = 24
SIDE = 4
GROUPS = 7
F32 = jnp.float32
BF16 = jnp.bfloat16
HIGHEST = lax.Precision.HIGHEST
VMEM_BYTES = 24 * 1024 * 1024


def iota(shape, dim):
    return lax.broadcasted_iota(jnp.int32, shape, dim)


def speed_of(index):
    return (index.astype(F32) - MIDDLE) / MIDDLE


def from_below_y(a):
    return pltpu.roll(a, NZ, 1)


def from_above_y(a):
    return pltpu.roll(a, CELLS - NZ, 1)


def from_below_z(a):
    first = iota(a.shape, 1) % NZ == 0
    return jnp.where(first, pltpu.roll(a, CELLS - (NZ - 1), 1), pltpu.roll(a, 1, 1))


def from_above_z(a):
    last = iota(a.shape, 1) % NZ == NZ - 1
    return jnp.where(last, pltpu.roll(a, NZ - 1, 1), pltpu.roll(a, CELLS - 1, 1))


def split(a, pieces):
    out = []
    for _ in range(pieces):
        out.append(a.astype(BF16))
        a = a - out[-1].astype(F32)
    return out


def three_sum(a):
    return a[0:8] + a[8:16] + a[16:24]


def node_rows(z_speed):
    node = iota((8, NODES), 1)
    k = iota((8, NODES), 0)
    x, y = speed_of(node % Q), speed_of(node // Q)
    z = jnp.broadcast_to(z_speed, (8, NODES))
    invariants = jnp.where(k == 0, 1.0, 0.0)
    for row, value in ((1, x), (2, y), (3, z), (4, x * x + y * y + z * z)):
        invariants = jnp.where(k == row, value, invariants)
    factors = [None]
    for speed in (x, y, z):
        factors.append(COURANT_SCALE * jnp.maximum(speed, 0.0))
        factors.append(COURANT_SCALE * jnp.maximum(-speed, 0.0))
    return invariants, factors


def weights_rows(z_speed, weight):
    invariants, factors = node_rows(z_speed)
    base = weight * invariants
    return invariants, base, jnp.concatenate([base] + [base * f for f in factors[1:]], axis=0)


def advected_rows(m, s, below, above, z_speed):
    row = iota((Q, CELLS), 0)
    lane = iota((Q, CELLS), 1)
    x_courant = COURANT_SCALE * jnp.abs(speed_of(row))
    y_courant = COURANT_SCALE * abs((m - MIDDLE) / MIDDLE)
    z_courant = COURANT_SCALE * jnp.abs(z_speed)
    up = z_speed > 0
    edge = jnp.where(up, 0, NZ - 1)
    near = pltpu.roll(s, jnp.where(up, 1, CELLS - 1), 1)
    far = pltpu.roll(s, jnp.where(up, CELLS - (NZ - 1), NZ - 1), 1)
    z_side = jnp.where(lane % NZ == edge, far, near)
    y_side = from_below_y(s) if m >= Q // 2 else from_above_y(s)
    x_side = jnp.concatenate([above, below], axis=0)
    flux = x_courant * (s - x_side) + y_courant * (s - y_side) + z_courant * (s - z_side)
    return s - flux


def equilibrium_rows(m, coeffs, z_speed):
    y = (m - MIDDLE) / MIDDLE
    x = speed_of(iota((Q, CELLS), 0))
    common = coeffs[0:1] + y * coeffs[2:3] + z_speed * coeffs[3:4]
    common = common + (y * y + z_speed * z_speed) * coeffs[4:5]
    return common + x * coeffs[1:2] + (x * x) * coeffs[4:5]


def apply_small(matrix, first, rows):
    total = matrix[:, first : first + 1] * rows[0:1]
    for k in range(1, 5):
        total = total + matrix[:, first + k : first + k + 1] * rows[k : k + 1]
    return total


def inverse_of(gram):
    row, lane = iota((8, 128), 0), iota((8, 128), 1)
    work = jnp.where((row < 5) & (lane < 5), gram, 0.0)
    work = jnp.where((lane == row + 8) | ((lane == row) & (row >= 5)), 1.0, work)
    for i in range(5):
        pivot = work[i : i + 1, :] / work[i : i + 1, i : i + 1]
        work = jnp.where(row == i, pivot, work - work[:, i : i + 1] * pivot)
    return work


def load_state(ref, m):
    halves = [ref[pl.ds(2 * Q * m + h, Q, stride=2), :] for h in range(2)]
    return jnp.concatenate(halves, axis=1)


def store_sides(m, s, low_ref, high_ref):
    low_ref[8 * m : 8 * m + 8, :] = s[0:8]
    high_ref[8 * m : 8 * m + 8, :] = s[8:16]


def copies_kernel(state_ref, copies_ref, low_ref, high_ref):
    for m in range(Q):
        s = load_state(state_ref, m)
        store_sides(m, s, low_ref, high_ref)
        rounded = s.astype(BF16)
        for part in range(SIDE):
            copies_ref[part * NODES + Q * m : part * NODES + Q * m + Q, :] = rounded


def arrival(place_ref, col):
    first, y, x = place_ref[0], place_ref[1], place_ref[2]
    from_y, from_x = col // (2 * SIDE), col // 2 % SIDE
    bundle = jnp.where(first == 0, y - from_y, x - from_x)
    bundle = jnp.where(bundle < 0, bundle + SIDE, bundle)
    return (bundle * SIDE + jnp.where(first == 0, from_x, from_y)) * 2 + col % 2


def prepare_kernel(
    cols_ref, place_ref, z_ref, weight_ref, tiles_ref, dense_ref, wk_out_ref, wk_ref, sem
):
    invariants, base, phi = weights_rows(z_ref[0], weight_ref[...])
    padded = jnp.concatenate([phi, jnp.zeros((TILE - 8 * GROUPS, NODES), F32)], axis=0)
    small = lax.dot_general(
        invariants, padded, (((1,), (1,)), ((), ())), precision=HIGHEST, preferred_element_type=F32
    )
    wk_ref[...] = jnp.zeros_like(wk_ref)
    dense_ref[...] = jnp.zeros_like(dense_ref)
    wk_ref[2 * PARTS] = small
    pieces = jnp.concatenate([p.astype(F32) for p in split(base, 3)], axis=0).astype(BF16)
    for r in range(2):
        part = three_sum(
            jnp.dot(pieces[:, r * TILE : (r + 1) * TILE], tiles_ref[r], preferred_element_type=F32)
        )
        for j in range(NB):
            at = slice(j * TILE, (j + 1) * TILE)
            col = cols_ref[r, j]
            wk_ref[col] = wk_ref[col] + part[:, at]
            where = pl.ds(pl.multiple_of(arrival(place_ref, col) * TILE, TILE), TILE)
            dense_ref[r * TILE : (r + 1) * TILE, where] = tiles_ref[r, :, at]
    copy = pltpu.make_async_copy(wk_ref, wk_out_ref, sem)
    copy.start()
    copy.wait()


def step_rows(rate, z_speed):
    keep = 1.0 / (1.0 + rate)
    rows = [KERNEL_STEP * keep, rate * keep, 1.0 + rate, jnp.full((1, CELLS), z_speed)]
    return jnp.concatenate(rows + [jnp.zeros((4, CELLS), F32)], axis=0)


def base_kernel(z_ref, state_ref, rate_ref, weight_ref, above_ref, below_ref, base_ref):
    z_speed = z_ref[0]
    rate = rate_ref[...]
    keep = 1.0 / (1.0 + rate)
    for m in range(Q):
        half = slice(8 * m, 8 * m + 8)
        s = load_state(state_ref, m)
        e = advected_rows(m, s, below_ref[half, :], above_ref[half, :], z_speed)
        base_ref[Q * m : Q * m + Q, :] = keep * e
    base_ref[NODES:, :] = step_rows(rate, z_speed)
    base_ref[NODES + 4 : NODES + 5, :] = weight_ref[...]


def kernel_product(dense_ref, bundle_refs, stride):
    total = None
    for i, ref in enumerate(bundle_refs):
        blocks = [ref[j * stride : j * stride + NODES, :] for j in range(SIDE)]
        at = slice(i * SIDE * NODES, (i + 1) * SIDE * NODES)
        part = jnp.dot(
            dense_ref[:, at], jnp.concatenate(blocks, axis=0), preferred_element_type=F32
        )
        total = part if total is None else total + part
    return total


def first_kernel(
    dense_ref, base_ref, own_ref, near_ref, far_ref, back_ref, wk_in_ref,
    scaled_ref, payload_ref, wk_ref, sem,
):
    copy = pltpu.make_async_copy(wk_in_ref, wk_ref, sem)
    copy.start()
    term = kernel_product(dense_ref, (own_ref, near_ref, far_ref, back_ref), NODES)
    scaled = base_ref[0:NODES, :] + base_ref[NODES : NODES + 1, :] * term
    scaled_ref[0:NODES, :] = scaled
    scaled_ref[NODES : NODES + 8, :] = base_ref[NODES:, :]
    rows = base_ref[NODES:, :]
    _, _, phi = weights_rows(rows[3:4], rows[4:5])
    moments = jnp.dot(phi, scaled, precision=HIGHEST, preferred_element_type=F32)
    group = [moments[8 * t : 8 * t + 8] for t in range(GROUPS)]
    flux = group[1] + group[2]
    for t, shift in ((3, from_below_y), (4, from_above_y), (5, from_below_z), (6, from_above_z)):
        flux = flux + (group[t] - shift(group[t]))
    scaled_ref[NODES + 8 :, :] = flux
    k = iota((8, CELLS), 0)
    first = group[0]
    second = jnp.where(k < 5, group[1], pltpu.roll(group[2], 6, 0))
    copy.wait()
    small = jnp.concatenate([wk_ref[2 * PARTS], jnp.zeros((8, CELLS - TILE), F32)], axis=1)
    third = jnp.where(k < 5, small, pltpu.roll(group[2], 3, 0))
    for part in range(PARTS):
        wk = jnp.concatenate([wk_ref[2 * part], wk_ref[2 * part + 1]], axis=1)
        start = part * PAYLOAD
        payload_ref[start : start + 8, :] = jnp.where(k < 5, first, pltpu.roll(wk, 5, 0))
        payload_ref[start + 8 : start + 16, :] = jnp.where(
            (k < 5) | (k == 7), second, pltpu.roll(wk, 2, 0)
        )
        payload_ref[start + 16 : start + 24, :] = third


def totals_of(payload_ref, scaled_ref):
    total = payload_ref[0:PAYLOAD, :]
    for part in range(1, PARTS):
        total = total + payload_ref[part * PAYLOAD : (part + 1) * PAYLOAD, :]
    first, second, third = total[0:8], total[8:16], total[16:24]
    k = iota((8, CELLS), 0)
    mine = k < 5
    wk = jnp.where(k < 3, pltpu.roll(first, 3, 0), jnp.where(mine, pltpu.roll(second, 6, 0), 0.0))
    down = jnp.where(k == 1, pltpu.roll(second, 2, 0), jnp.where(mine, pltpu.roll(third, 5, 0), 0.0))
    down = jnp.where(k == 0, second - COURANT_SCALE * pltpu.roll(first, 7, 0), down)
    first, second, small = [jnp.where(mine, g, 0.0) for g in (first, second, third)]
    inverse = inverse_of(small[:, 0:128])
    rows = scaled_ref[NODES : NODES + 8, :]
    coeffs = rows[1:2] * apply_small(inverse, 8, rows[2:3] * first)
    return (first, second, down), wk, small, inverse, coeffs


def middle_kernel(payload_ref, scaled_ref, copies_ref, block_ref):
    group, wk, small, inverse, coeffs = totals_of(payload_ref, scaled_ref)
    z_speed = scaled_ref[NODES + 3 : NODES + 4, :]
    for m in range(Q):
        rows = slice(Q * m, Q * m + Q)
        s = scaled_ref[rows, :] + equilibrium_rows(m, coeffs, z_speed)
        rounded = s.astype(BF16)
        block_ref[rows, :] = rounded
        for part in range(SIDE):
            start = part * (NODES + EXTRA) + Q * m
            copies_ref[start : start + Q, :] = rounded
    pieces = jnp.concatenate([p.astype(F32) for p in split(wk, 3)], axis=0).astype(BF16)
    own = KERNEL_STEP * three_sum(jnp.dot(pieces, block_ref[...], preferred_element_type=F32))
    own = own - scaled_ref[NODES + 8 :, :]
    own = jnp.concatenate([p.astype(F32) for p in split(own, 2)], axis=0).astype(BF16)
    for part in range(SIDE):
        start = part * (NODES + EXTRA) + NODES
        copies_ref[start : start + EXTRA, :] = own


def state_kernel(payload_ref, scaled_ref, state_ref, low_ref, high_ref):
    group, wk, small, inverse, coeffs = totals_of(payload_ref, scaled_ref)
    z_speed = scaled_ref[NODES + 3 : NODES + 4, :]
    from_eq = [apply_small(small, 8 * t, coeffs) for t in range(GROUPS)]
    flux = from_eq[1] + from_eq[2]
    for t, shift in ((3, from_below_y), (4, from_above_y), (5, from_below_z), (6, from_above_z)):
        flux = flux + (from_eq[t] - shift(from_eq[t]))
    high_ref[NODES // 2 :, :] = group[1] + from_eq[1]
    low_ref[NODES // 2 :, :] = group[2] + from_eq[2]
    for m in range(Q):
        rows = slice(Q * m, Q * m + Q)
        s = scaled_ref[rows, :] + equilibrium_rows(m, coeffs, z_speed)
        state_ref[rows, :] = s
        store_sides(m, s, low_ref, high_ref)
    state_ref[NODES : NODES + 8, :] = group[0] + from_eq[0] - flux
    state_ref[NODES + 8 :, :] = jnp.concatenate([inverse, inverse], axis=1)


def second_base_kernel(z_ref, state_ref, rate_ref, above_ref, below_ref, base_ref):
    z_speed = z_ref[0]
    rate = rate_ref[...]
    keep = 1.0 / (1.0 + rate)
    for m in range(Q):
        rows = slice(Q * m, Q * m + Q)
        half = slice(8 * m, 8 * m + 8)
        e = advected_rows(m, state_ref[rows, :], below_ref[half, :], above_ref[half, :], z_speed)
        base_ref[rows, :] = keep * e
    sides_part = above_ref[NODES // 2 :, :] + below_ref[NODES // 2 :, :]
    base_ref[NODES : NODES + 8, :] = state_ref[NODES : NODES + 8, :] + sides_part
    base_ref[NODES + 8 : NODES + 16, :] = state_ref[NODES + 8 : NODES + 16, :]
    base_ref[NODES + 16 :, :] = step_rows(rate, z_speed)


def last_kernel(dense_ref, base_ref, own_ref, near_ref, far_ref, back_ref, out_ref, term_ref):
    stride = NODES + EXTRA
    bundles = (own_ref, near_ref, far_ref, back_ref)
    term_ref[...] = kernel_product(dense_ref, bundles, stride)
    total = base_ref[NODES : NODES + 8, :]
    for ref in bundles:
        for j in range(SIDE):
            own = ref[j * stride + NODES : (j + 1) * stride, :].astype(F32)
            total = total + (own[0:8] + own[8:16])
    rows = base_ref[NODES + 16 :, :]
    coeffs = rows[1:2] * apply_small(base_ref[NODES + 8 : NODES + 16, 0:128], 8, total)
    for m in range(Q):
        at = slice(Q * m, Q * m + Q)
        new = base_ref[at, :] + rows[0:1] * term_ref[at, :] + equilibrium_rows(m, coeffs, rows[3:4])
        for h in range(2):
            out_ref[pl.ds(2 * Q * m + h, Q, stride=2), :] = new[:, 128 * h : 128 * h + 128]


VMEM = pl.BlockSpec(memory_space=pltpu.VMEM)
SMEM = pl.BlockSpec(memory_space=pltpu.SMEM)
HBM = pl.BlockSpec(memory_space=pltpu.HBM)


def call(kernel, scalars, arrays, outs, scratch=(), in_hbm=(), from_hbm=()):
    from_hbm = [pltpu.with_memory_space_constraint(a, pltpu.HBM) for a in from_hbm]
    return pl.pallas_call(
        kernel,
        out_shape=[
            (pltpu.HBM if i in in_hbm else jax.ShapeDtypeStruct)(shape, kind) for i, (shape, kind) in enumerate(outs)
        ],
        in_specs=[SMEM] * len(scalars) + [VMEM] * len(arrays) + [HBM] * len(from_hbm),
        out_specs=[HBM if i in in_hbm else VMEM for i in range(len(outs))],
        scratch_shapes=list(scratch),
        compiler_params=pltpu.CompilerParams(vmem_limit_bytes=VMEM_BYTES),
    )(*scalars, *arrays, *from_hbm)


def sides(low, high):
    count = lax.axis_size("gx")
    up = [(i, (i + 1) % count) for i in range(count)]
    down = [(target, source) for source, target in up]
    return lax.ppermute(low, "gx", down), lax.ppermute(high, "gx", up)


def spread(copies):
    return lax.all_to_all(copies, "vert", 0, 0, tiled=True)


def gather(copies):
    slabs = lax.axis_size("gx")
    groups, pairs = [], [[], [], []]
    for g in range(slabs):
        for i in range(SIDE):
            line = [i * SIDE + j if g % 2 == 0 else j * SIDE + i for j in range(SIDE)]
            groups.append([g * PARTS + v for v in line])
            for j in range(SIDE):
                for shift in (1, 2, 3):
                    y, x = (i + shift) % SIDE, j
                    ends = (i * SIDE + j, y * SIDE + x) if g % 2 == 0 else (j * SIDE + i, x * SIDE + y)
                    pairs[shift - 1].append(tuple(g * PARTS + v for v in ends))
    axes = ("gx", "vert")
    bundle = lax.all_to_all(copies, axes, 0, 0, axis_index_groups=groups, tiled=True)
    return [bundle] + [lax.ppermute(bundle, axes, p) for p in pairs]


def per_device(distribution, relax_rate, node_weight, kernel_tiles, tile_cols):
    state = distribution.reshape(2 * NODES, CELLS // 2)
    weight = node_weight.reshape(1, NODES)
    z_speed = speed_of(lax.axis_index("vert")).reshape(1)
    half = NODES // 2
    vert = lax.axis_index("vert")
    place = jnp.stack([lax.axis_index("gx") % 2, vert // SIDE, vert % SIDE]).astype(jnp.int32)
    wk_rows = (2 * PARTS + 1, 8, TILE)
    dma = pltpu.SemaphoreType.DMA
    copies, low, high = call(
        copies_kernel, [], [state],
        [((SIDE * NODES, CELLS), BF16), ((half, CELLS), F32), ((half, CELLS), F32)],
    )
    bundles = gather(copies)
    dense, wk = call(
        prepare_kernel, [tile_cols, place, z_speed], [weight, kernel_tiles],
        [((NODES, PARTS * NODES), BF16), (wk_rows, F32)], [pltpu.VMEM(wk_rows, F32), dma], (1,),
    )
    above, below = sides(low, high)
    (base,) = call(
        base_kernel, [z_speed], [state, relax_rate, weight, above, below], [((NODES + 8, CELLS), F32)]
    )
    scaled, payload = call(
        first_kernel, [], [dense, base, *bundles],
        [((NODES + 16, CELLS), F32), ((PARTS * PAYLOAD, CELLS), F32)],
        [pltpu.VMEM(wk_rows, F32), dma], (), [wk],
    )
    payload = spread(payload)
    (copies,) = call(
        middle_kernel, [], [payload, scaled], [((SIDE * (NODES + EXTRA), CELLS), BF16)],
        [pltpu.VMEM((NODES, CELLS), BF16)],
    )
    bundles = gather(copies)
    state, low, high = call(
        state_kernel, [], [payload, scaled],
        [((NODES + 16, CELLS), F32), ((half + 8, CELLS), F32), ((half + 8, CELLS), F32)],
    )
    above, below = sides(low, high)
    (base,) = call(
        second_base_kernel, [z_speed], [state, relax_rate, above, below],
        [((NODES + 24, CELLS), F32)],
    )
    (out,) = call(
        last_kernel, [], [dense, base, *bundles], [((2 * NODES, CELLS // 2), F32)],
        [pltpu.VMEM((NODES, CELLS), F32)],
    )
    return out.reshape(distribution.shape)


def solution(mesh):
    placed = (
        P("vert", "gx", None),
        P("gx", None),
        P("vert"),
        P("vert", None, None),
        P("vert", None),
    )
    return jax.shard_map(
        per_device, mesh=mesh, in_specs=placed, out_specs=P("vert", "gx", None), check_vma=False
    )
```

```python
import functools

import jax
import jax.numpy as jnp
from jax import lax
from jax.experimental import pallas as pl
from jax.experimental.pallas import tpu as pltpu
from jax.sharding import PartitionSpec as P

Q = 16
TILE = 128
NB = 12
NZ = 4
CELLS = 256
NODES = 256
PARTS = 16
COURANT_SCALE = 0.3
KERNEL_STEP = 0.5
MIDDLE = (Q - 1) / 2.0
EXTRA = 16
PAYLOAD = 24
SIDE = 4
GROUPS = 7
F32 = jnp.float32
BF16 = jnp.bfloat16
HIGHEST = lax.Precision.HIGHEST
VMEM_BYTES = 24 * 1024 * 1024


def iota(shape, dim):
    return lax.broadcasted_iota(jnp.int32, shape, dim)


def speed_of(index):
    return (index.astype(F32) - MIDDLE) / MIDDLE


def from_below_y(a):
    return pltpu.roll(a, NZ, 1)


def from_above_y(a):
    return pltpu.roll(a, CELLS - NZ, 1)


def from_below_z(a):
    first = iota(a.shape, 1) % NZ == 0
    return jnp.where(first, pltpu.roll(a, CELLS - (NZ - 1), 1), pltpu.roll(a, 1, 1))


def from_above_z(a):
    last = iota(a.shape, 1) % NZ == NZ - 1
    return jnp.where(last, pltpu.roll(a, NZ - 1, 1), pltpu.roll(a, CELLS - 1, 1))


def split(a, pieces):
    out = []
    for _ in range(pieces):
        out.append(a.astype(BF16))
        a = a - out[-1].astype(F32)
    return out


def three_sum(a):
    return a[0:8] + a[8:16] + a[16:24]


def node_rows(z_speed):
    node = iota((8, NODES), 1)
    k = iota((8, NODES), 0)
    x, y = speed_of(node % Q), speed_of(node // Q)
    z = jnp.broadcast_to(z_speed, (8, NODES))
    invariants = jnp.where(k == 0, 1.0, 0.0)
    for row, value in ((1, x), (2, y), (3, z), (4, x * x + y * y + z * z)):
        invariants = jnp.where(k == row, value, invariants)
    factors = [None]
    for speed in (x, y, z):
        factors.append(COURANT_SCALE * jnp.maximum(speed, 0.0))
        factors.append(COURANT_SCALE * jnp.maximum(-speed, 0.0))
    return invariants, factors


def weights_rows(z_speed, weight):
    invariants, factors = node_rows(z_speed)
    base = weight * invariants
    return invariants, base, jnp.concatenate([base] + [base * f for f in factors[1:]], axis=0)


def advected_rows(m, s, below, above, z_speed):
    row = iota((Q, CELLS), 0)
    lane = iota((Q, CELLS), 1)
    x_courant = COURANT_SCALE * jnp.abs(speed_of(row))
    y_courant = COURANT_SCALE * abs((m - MIDDLE) / MIDDLE)
    z_courant = COURANT_SCALE * jnp.abs(z_speed)
    up = z_speed > 0
    edge = jnp.where(up, 0, NZ - 1)
    near = pltpu.roll(s, jnp.where(up, 1, CELLS - 1), 1)
    far = pltpu.roll(s, jnp.where(up, CELLS - (NZ - 1), NZ - 1), 1)
    z_side = jnp.where(lane % NZ == edge, far, near)
    y_side = from_below_y(s) if m >= Q // 2 else from_above_y(s)
    x_side = jnp.concatenate([above, below], axis=0)
    flux = x_courant * (s - x_side) + y_courant * (s - y_side) + z_courant * (s - z_side)
    return s - flux


def equilibrium_rows(m, coeffs, z_speed):
    y = (m - MIDDLE) / MIDDLE
    x = speed_of(iota((Q, CELLS), 0))
    common = coeffs[0:1] + y * coeffs[2:3] + z_speed * coeffs[3:4]
    common = common + (y * y + z_speed * z_speed) * coeffs[4:5]
    return common + x * coeffs[1:2] + (x * x) * coeffs[4:5]


def apply_small(matrix, first, rows):
    total = matrix[:, first : first + 1] * rows[0:1]
    for k in range(1, 5):
        total = total + matrix[:, first + k : first + k + 1] * rows[k : k + 1]
    return total


def inverse_of(gram):
    row, lane = iota((8, 128), 0), iota((8, 128), 1)
    work = jnp.where((row < 5) & (lane < 5), gram, 0.0)
    work = jnp.where((lane == row + 8) | ((lane == row) & (row >= 5)), 1.0, work)
    for i in range(5):
        pivot = work[i : i + 1, :] / work[i : i + 1, i : i + 1]
        work = jnp.where(row == i, pivot, work - work[:, i : i + 1] * pivot)
    return work


def load_state(ref, m):
    halves = [ref[pl.ds(2 * Q * m + h, Q, stride=2), :] for h in range(2)]
    return jnp.concatenate(halves, axis=1)


def store_sides(m, s, low_ref, high_ref):
    low_ref[8 * m : 8 * m + 8, :] = s[0:8]
    high_ref[8 * m : 8 * m + 8, :] = s[8:16]


def copies_kernel(state_ref, copies_ref, low_ref, high_ref):
    for m in range(Q):
        s = load_state(state_ref, m)
        store_sides(m, s, low_ref, high_ref)
        rounded = s.astype(BF16)
        for part in range(SIDE):
            copies_ref[part * NODES + Q * m : part * NODES + Q * m + Q, :] = rounded


def arrival(place_ref, col):
    first, y, x = place_ref[0], place_ref[1], place_ref[2]
    from_y, from_x = col // (2 * SIDE), col // 2 % SIDE
    bundle = jnp.where(first == 0, y - from_y, x - from_x)
    bundle = jnp.where(bundle < 0, bundle + SIDE, bundle)
    return (bundle * SIDE + jnp.where(first == 0, from_x, from_y)) * 2 + col % 2


def prepare_kernel(
    cols_ref, place_ref, z_ref, weight_ref, tiles_ref, dense_ref, wk_out_ref, wk_ref, sem
):
    invariants, base, phi = weights_rows(z_ref[0], weight_ref[...])
    padded = jnp.concatenate([phi, jnp.zeros((TILE - 8 * GROUPS, NODES), F32)], axis=0)
    small = lax.dot_general(
        invariants, padded, (((1,), (1,)), ((), ())), precision=HIGHEST, preferred_element_type=F32
    )
    wk_ref[...] = jnp.zeros_like(wk_ref)
    dense_ref[...] = jnp.zeros_like(dense_ref)
    wk_ref[2 * PARTS] = small
    pieces = jnp.concatenate([p.astype(F32) for p in split(base, 3)], axis=0).astype(BF16)
    for r in range(2):
        part = three_sum(
            jnp.dot(pieces[:, r * TILE : (r + 1) * TILE], tiles_ref[r], preferred_element_type=F32)
        )
        for j in range(NB):
            at = slice(j * TILE, (j + 1) * TILE)
            col = cols_ref[r, j]
            wk_ref[col] = wk_ref[col] + part[:, at]
            where = pl.ds(pl.multiple_of(arrival(place_ref, col) * TILE, TILE), TILE)
            dense_ref[r * TILE : (r + 1) * TILE, where] = tiles_ref[r, :, at]
    copy = pltpu.make_async_copy(wk_ref, wk_out_ref, sem)
    copy.start()
    copy.wait()


def step_rows(rate, z_speed):
    keep = 1.0 / (1.0 + rate)
    rows = [KERNEL_STEP * keep, rate * keep, 1.0 + rate, jnp.full((1, CELLS), z_speed)]
    return jnp.concatenate(rows + [jnp.zeros((4, CELLS), F32)], axis=0)


def base_kernel(z_ref, state_ref, rate_ref, weight_ref, above_ref, below_ref, base_ref):
    z_speed = z_ref[0]
    rate = rate_ref[...]
    keep = 1.0 / (1.0 + rate)
    for m in range(Q):
        half = slice(8 * m, 8 * m + 8)
        s = load_state(state_ref, m)
        e = advected_rows(m, s, below_ref[half, :], above_ref[half, :], z_speed)
        base_ref[Q * m : Q * m + Q, :] = keep * e
    base_ref[NODES:, :] = step_rows(rate, z_speed)
    base_ref[NODES + 4 : NODES + 5, :] = weight_ref[...]


def kernel_product(dense_ref, bundle_refs, stride):
    total = None
    for i, ref in enumerate(bundle_refs):
        blocks = [ref[j * stride : j * stride + NODES, :] for j in range(SIDE)]
        at = slice(i * SIDE * NODES, (i + 1) * SIDE * NODES)
        part = jnp.dot(
            dense_ref[:, at], jnp.concatenate(blocks, axis=0), preferred_element_type=F32
        )
        total = part if total is None else total + part
    return total


def first_kernel(
    dense_ref, base_ref, own_ref, near_ref, far_ref, back_ref, wk_in_ref,
    scaled_ref, payload_ref, wk_ref, sem,
):
    copy = pltpu.make_async_copy(wk_in_ref, wk_ref, sem)
    copy.start()
    term = kernel_product(dense_ref, (own_ref, near_ref, far_ref, back_ref), NODES)
    scaled = base_ref[0:NODES, :] + base_ref[NODES : NODES + 1, :] * term
    scaled_ref[0:NODES, :] = scaled
    scaled_ref[NODES : NODES + 8, :] = base_ref[NODES:, :]
    rows = base_ref[NODES:, :]
    _, _, phi = weights_rows(rows[3:4], rows[4:5])
    moments = jnp.dot(phi, scaled, precision=HIGHEST, preferred_element_type=F32)
    group = [moments[8 * t : 8 * t + 8] for t in range(GROUPS)]
    flux = group[1] + group[2]
    for t, shift in ((3, from_below_y), (4, from_above_y), (5, from_below_z), (6, from_above_z)):
        flux = flux + (group[t] - shift(group[t]))
    scaled_ref[NODES + 8 :, :] = flux
    k = iota((8, CELLS), 0)
    first = group[0]
    second = jnp.where(k < 5, group[1], pltpu.roll(group[2], 6, 0))
    copy.wait()
    small = jnp.concatenate([wk_ref[2 * PARTS], jnp.zeros((8, CELLS - TILE), F32)], axis=1)
    third = jnp.where(k < 5, small, pltpu.roll(group[2], 3, 0))
    for part in range(PARTS):
        wk = jnp.concatenate([wk_ref[2 * part], wk_ref[2 * part + 1]], axis=1)
        start = part * PAYLOAD
        payload_ref[start : start + 8, :] = jnp.where(k < 5, first, pltpu.roll(wk, 5, 0))
        payload_ref[start + 8 : start + 16, :] = jnp.where(
            (k < 5) | (k == 7), second, pltpu.roll(wk, 2, 0)
        )
        payload_ref[start + 16 : start + 24, :] = third


def totals_of(payload_ref, scaled_ref):
    total = payload_ref[0:PAYLOAD, :]
    for part in range(1, PARTS):
        total = total + payload_ref[part * PAYLOAD : (part + 1) * PAYLOAD, :]
    first, second, third = total[0:8], total[8:16], total[16:24]
    k = iota((8, CELLS), 0)
    mine = k < 5
    wk = jnp.where(k < 3, pltpu.roll(first, 3, 0), jnp.where(mine, pltpu.roll(second, 6, 0), 0.0))
    down = jnp.where(k == 1, pltpu.roll(second, 2, 0), jnp.where(mine, pltpu.roll(third, 5, 0), 0.0))
    down = jnp.where(k == 0, second - COURANT_SCALE * pltpu.roll(first, 7, 0), down)
    first, second, small = [jnp.where(mine, g, 0.0) for g in (first, second, third)]
    inverse = inverse_of(small[:, 0:128])
    rows = scaled_ref[NODES : NODES + 8, :]
    coeffs = rows[1:2] * apply_small(inverse, 8, rows[2:3] * first)
    return (first, second, down), wk, small, inverse, coeffs


def middle_kernel(payload_ref, scaled_ref, copies_ref, block_ref):
    group, wk, small, inverse, coeffs = totals_of(payload_ref, scaled_ref)
    z_speed = scaled_ref[NODES + 3 : NODES + 4, :]
    for m in range(Q):
        rows = slice(Q * m, Q * m + Q)
        s = scaled_ref[rows, :] + equilibrium_rows(m, coeffs, z_speed)
        rounded = s.astype(BF16)
        block_ref[rows, :] = rounded
        for part in range(SIDE):
            start = part * (NODES + EXTRA) + Q * m
            copies_ref[start : start + Q, :] = rounded
    pieces = jnp.concatenate([p.astype(F32) for p in split(wk, 3)], axis=0).astype(BF16)
    own = KERNEL_STEP * three_sum(jnp.dot(pieces, block_ref[...], preferred_element_type=F32))
    own = own - scaled_ref[NODES + 8 :, :]
    own = jnp.concatenate([p.astype(F32) for p in split(own, 2)], axis=0).astype(BF16)
    for part in range(SIDE):
        start = part * (NODES + EXTRA) + NODES
        copies_ref[start : start + EXTRA, :] = own


def state_kernel(payload_ref, scaled_ref, state_ref, low_ref, high_ref):
    group, wk, small, inverse, coeffs = totals_of(payload_ref, scaled_ref)
    z_speed = scaled_ref[NODES + 3 : NODES + 4, :]
    from_eq = [apply_small(small, 8 * t, coeffs) for t in range(GROUPS)]
    flux = from_eq[1] + from_eq[2]
    for t, shift in ((3, from_below_y), (4, from_above_y), (5, from_below_z), (6, from_above_z)):
        flux = flux + (from_eq[t] - shift(from_eq[t]))
    high_ref[NODES // 2 :, :] = group[1] + from_eq[1]
    low_ref[NODES // 2 :, :] = group[2] + from_eq[2]
    for m in range(Q):
        rows = slice(Q * m, Q * m + Q)
        s = scaled_ref[rows, :] + equilibrium_rows(m, coeffs, z_speed)
        state_ref[rows, :] = s
        store_sides(m, s, low_ref, high_ref)
    state_ref[NODES : NODES + 8, :] = group[0] + from_eq[0] - flux
    state_ref[NODES + 8 :, :] = jnp.concatenate([inverse, inverse], axis=1)


def second_base_kernel(z_ref, state_ref, rate_ref, above_ref, below_ref, base_ref):
    z_speed = z_ref[0]
    rate = rate_ref[...]
    keep = 1.0 / (1.0 + rate)
    for m in range(Q):
        rows = slice(Q * m, Q * m + Q)
        half = slice(8 * m, 8 * m + 8)
        e = advected_rows(m, state_ref[rows, :], below_ref[half, :], above_ref[half, :], z_speed)
        base_ref[rows, :] = keep * e
    sides_part = above_ref[NODES // 2 :, :] + below_ref[NODES // 2 :, :]
    base_ref[NODES : NODES + 8, :] = state_ref[NODES : NODES + 8, :] + sides_part
    base_ref[NODES + 8 : NODES + 16, :] = state_ref[NODES + 8 : NODES + 16, :]
    base_ref[NODES + 16 :, :] = step_rows(rate, z_speed)


def last_kernel(dense_ref, base_ref, own_ref, near_ref, far_ref, back_ref, out_ref, term_ref):
    stride = NODES + EXTRA
    bundles = (own_ref, near_ref, far_ref, back_ref)
    term_ref[...] = kernel_product(dense_ref, bundles, stride)
    total = base_ref[NODES : NODES + 8, :]
    for ref in bundles:
        for j in range(SIDE):
            own = ref[j * stride + NODES : (j + 1) * stride, :].astype(F32)
            total = total + (own[0:8] + own[8:16])
    rows = base_ref[NODES + 16 :, :]
    coeffs = rows[1:2] * apply_small(base_ref[NODES + 8 : NODES + 16, 0:128], 8, total)
    for m in range(Q):
        at = slice(Q * m, Q * m + Q)
        new = base_ref[at, :] + rows[0:1] * term_ref[at, :] + equilibrium_rows(m, coeffs, rows[3:4])
        for h in range(2):
            out_ref[pl.ds(2 * Q * m + h, Q, stride=2), :] = new[:, 128 * h : 128 * h + 128]


VMEM = pl.BlockSpec(memory_space=pltpu.VMEM)
SMEM = pl.BlockSpec(memory_space=pltpu.SMEM)
HBM = pl.BlockSpec(memory_space=pltpu.HBM)


def call(kernel, scalars, arrays, outs, scratch=(), in_hbm=(), from_hbm=()):
    from_hbm = [pltpu.with_memory_space_constraint(a, pltpu.HBM) for a in from_hbm]
    return pl.pallas_call(
        kernel,
        out_shape=[
            (pltpu.HBM if i in in_hbm else jax.ShapeDtypeStruct)(shape, kind) for i, (shape, kind) in enumerate(outs)
        ],
        in_specs=[SMEM] * len(scalars) + [VMEM] * len(arrays) + [HBM] * len(from_hbm),
        out_specs=[HBM if i in in_hbm else VMEM for i in range(len(outs))],
        scratch_shapes=list(scratch),
        compiler_params=pltpu.CompilerParams(vmem_limit_bytes=VMEM_BYTES),
    )(*scalars, *arrays, *from_hbm)


def sides(low, high):
    count = lax.axis_size("gx")
    up = [(i, (i + 1) % count) for i in range(count)]
    down = [(target, source) for source, target in up]
    return lax.ppermute(low, "gx", down), lax.ppermute(high, "gx", up)


def spread(copies):
    return lax.all_to_all(copies, "vert", 0, 0, tiled=True)


def gather(copies):
    slabs = lax.axis_size("gx")
    groups, pairs = [], [[], [], []]
    for g in range(slabs):
        for i in range(SIDE):
            line = [i * SIDE + j if g % 2 == 1 else j * SIDE + i for j in range(SIDE)]
            groups.append([g * PARTS + v for v in line])
            for j in range(SIDE):
                for shift in (1, 2, 3):
                    y, x = (i + shift) % SIDE, j
                    ends = (i * SIDE + j, y * SIDE + x) if g % 2 == 1 else (j * SIDE + i, x * SIDE + y)
                    pairs[shift - 1].append(tuple(g * PARTS + v for v in ends))
    axes = ("gx", "vert")
    bundle = lax.all_to_all(copies, axes, 0, 0, axis_index_groups=groups, tiled=True)
    return [bundle] + [lax.ppermute(bundle, axes, p) for p in pairs]


def per_device(distribution, relax_rate, node_weight, kernel_tiles, tile_cols):
    state = distribution.reshape(2 * NODES, CELLS // 2)
    weight = node_weight.reshape(1, NODES)
    z_speed = speed_of(lax.axis_index("vert")).reshape(1)
    half = NODES // 2
    vert = lax.axis_index("vert")
    place = jnp.stack([1 - lax.axis_index("gx") % 2, vert // SIDE, vert % SIDE]).astype(jnp.int32)
    wk_rows = (2 * PARTS + 1, 8, TILE)
    dma = pltpu.SemaphoreType.DMA
    copies, low, high = call(
        copies_kernel, [], [state],
        [((SIDE * NODES, CELLS), BF16), ((half, CELLS), F32), ((half, CELLS), F32)],
    )
    bundles = gather(copies)
    dense, wk = call(
        prepare_kernel, [tile_cols, place, z_speed], [weight, kernel_tiles],
        [((NODES, PARTS * NODES), BF16), (wk_rows, F32)], [pltpu.VMEM(wk_rows, F32), dma], (1,),
    )
    above, below = sides(low, high)
    (base,) = call(
        base_kernel, [z_speed], [state, relax_rate, weight, above, below], [((NODES + 8, CELLS), F32)]
    )
    scaled, payload = call(
        first_kernel, [], [dense, base, *bundles],
        [((NODES + 16, CELLS), F32), ((PARTS * PAYLOAD, CELLS), F32)],
        [pltpu.VMEM(wk_rows, F32), dma], (), [wk],
    )
    payload = spread(payload)
    (copies,) = call(
        middle_kernel, [], [payload, scaled], [((SIDE * (NODES + EXTRA), CELLS), BF16)],
        [pltpu.VMEM((NODES, CELLS), BF16)],
    )
    bundles = gather(copies)
    state, low, high = call(
        state_kernel, [], [payload, scaled],
        [((NODES + 16, CELLS), F32), ((half + 8, CELLS), F32), ((half + 8, CELLS), F32)],
    )
    above, below = sides(low, high)
    (base,) = call(
        second_base_kernel, [z_speed], [state, relax_rate, above, below],
        [((NODES + 24, CELLS), F32)],
    )
    (out,) = call(
        last_kernel, [], [dense, base, *bundles], [((2 * NODES, CELLS // 2), F32)],
        [pltpu.VMEM((NODES, CELLS), F32)],
    )
    return out.reshape(distribution.shape)


def solution(mesh):
    placed = (
        P("vert", "gx", None),
        P("gx", None),
        P("vert"),
        P("vert", None, None),
        P("vert", None),
    )
    return jax.shard_map(
        per_device, mesh=mesh, in_specs=placed, out_specs=P("vert", "gx", None), check_vma=False
    )
```

```python
import functools

import jax
import jax.numpy as jnp
from jax import lax
from jax.experimental import pallas as pl
from jax.experimental.pallas import tpu as pltpu
from jax.sharding import PartitionSpec as P

Q = 16
TILE = 128
NB = 12
NZ = 4
CELLS = 256
NODES = 256
PARTS = 16
COURANT_SCALE = 0.3
KERNEL_STEP = 0.5
MIDDLE = (Q - 1) / 2.0
EXTRA = 16
PAYLOAD = 24
OUT_STEP = 4
SIDE = 4
GROUPS = 7
F32 = jnp.float32
BF16 = jnp.bfloat16
HIGHEST = lax.Precision.HIGHEST
VMEM_BYTES = 24 * 1024 * 1024


def iota(shape, dim):
    return lax.broadcasted_iota(jnp.int32, shape, dim)


def speed_of(index):
    return (index.astype(F32) - MIDDLE) / MIDDLE


def from_below_y(a):
    return pltpu.roll(a, NZ, 1)


def from_above_y(a):
    return pltpu.roll(a, CELLS - NZ, 1)


def from_below_z(a):
    first = iota(a.shape, 1) % NZ == 0
    return jnp.where(first, pltpu.roll(a, CELLS - (NZ - 1), 1), pltpu.roll(a, 1, 1))


def from_above_z(a):
    last = iota(a.shape, 1) % NZ == NZ - 1
    return jnp.where(last, pltpu.roll(a, NZ - 1, 1), pltpu.roll(a, CELLS - 1, 1))


def split(a, pieces):
    out = []
    for _ in range(pieces):
        out.append(a.astype(BF16))
        a = a - out[-1].astype(F32)
    return out


def three_sum(a):
    return a[0:8] + a[8:16] + a[16:24]


def node_rows(z_speed):
    node = iota((8, NODES), 1)
    k = iota((8, NODES), 0)
    x, y = speed_of(node % Q), speed_of(node // Q)
    z = jnp.broadcast_to(z_speed, (8, NODES))
    invariants = jnp.where(k == 0, 1.0, 0.0)
    for row, value in ((1, x), (2, y), (3, z), (4, x * x + y * y + z * z)):
        invariants = jnp.where(k == row, value, invariants)
    factors = [None]
    for speed in (x, y, z):
        factors.append(COURANT_SCALE * jnp.maximum(speed, 0.0))
        factors.append(COURANT_SCALE * jnp.maximum(-speed, 0.0))
    return invariants, factors


def weights_rows(z_speed, weight):
    invariants, factors = node_rows(z_speed)
    base = weight * invariants
    return invariants, base, jnp.concatenate([base] + [base * f for f in factors[1:]], axis=0)


def advected_rows(m, s, below, above, z_speed):
    row = iota((Q, CELLS), 0)
    lane = iota((Q, CELLS), 1)
    x_courant = COURANT_SCALE * jnp.abs(speed_of(row))
    y_courant = COURANT_SCALE * abs((m - MIDDLE) / MIDDLE)
    z_courant = COURANT_SCALE * jnp.abs(z_speed)
    up = z_speed > 0
    edge = jnp.where(up, 0, NZ - 1)
    near = pltpu.roll(s, jnp.where(up, 1, CELLS - 1), 1)
    far = pltpu.roll(s, jnp.where(up, CELLS - (NZ - 1), NZ - 1), 1)
    z_side = jnp.where(lane % NZ == edge, far, near)
    y_side = from_below_y(s) if m >= Q // 2 else from_above_y(s)
    x_side = jnp.concatenate([above, below], axis=0)
    flux = x_courant * (s - x_side) + y_courant * (s - y_side) + z_courant * (s - z_side)
    return s - flux


def equilibrium_rows(m, coeffs, z_speed):
    y = (m - MIDDLE) / MIDDLE
    x = speed_of(iota((Q, CELLS), 0))
    common = coeffs[0:1] + y * coeffs[2:3] + z_speed * coeffs[3:4]
    common = common + (y * y + z_speed * z_speed) * coeffs[4:5]
    return common + x * coeffs[1:2] + (x * x) * coeffs[4:5]


def apply_small(matrix, first, rows):
    total = matrix[:, first : first + 1] * rows[0:1]
    for k in range(1, 5):
        total = total + matrix[:, first + k : first + k + 1] * rows[k : k + 1]
    return total


def inverse_of(gram):
    row, lane = iota((8, 128), 0), iota((8, 128), 1)
    work = jnp.where((row < 5) & (lane < 5), gram, 0.0)
    work = jnp.where((lane == row + 8) | ((lane == row) & (row >= 5)), 1.0, work)
    for i in range(5):
        pivot = work[i : i + 1, :] / work[i : i + 1, i : i + 1]
        work = jnp.where(row == i, pivot, work - work[:, i : i + 1] * pivot)
    return work


def load_state(ref, m):
    halves = [ref[pl.ds(2 * Q * m + h, Q, stride=2), :] for h in range(2)]
    return jnp.concatenate(halves, axis=1)


def store_sides(m, s, low_ref, high_ref):
    low_ref[8 * m : 8 * m + 8, :] = s[0:8]
    high_ref[8 * m : 8 * m + 8, :] = s[8:16]


def copies_kernel(state_ref, copies_ref, low_ref, high_ref):
    for m in range(Q):
        s = load_state(state_ref, m)
        store_sides(m, s, low_ref, high_ref)
        rounded = s.astype(BF16)
        for part in range(SIDE):
            copies_ref[part * NODES + Q * m : part * NODES + Q * m + Q, :] = rounded


def arrival(place_ref, col):
    first, y, x = place_ref[0], place_ref[1], place_ref[2]
    from_y, from_x = col // (2 * SIDE), col // 2 % SIDE
    bundle = jnp.where(first == 0, y - from_y, x - from_x)
    bundle = jnp.where(bundle < 0, bundle + SIDE, bundle)
    return (bundle * SIDE + jnp.where(first == 0, from_x, from_y)) * 2 + col % 2


def prepare_kernel(
    cols_ref, place_ref, z_ref, weight_ref, tiles_ref, dense_ref, wk_out_ref, wk_ref, sem
):
    invariants, base, phi = weights_rows(z_ref[0], weight_ref[...])
    padded = jnp.concatenate([phi, jnp.zeros((TILE - 8 * GROUPS, NODES), F32)], axis=0)
    small = lax.dot_general(
        invariants, padded, (((1,), (1,)), ((), ())), precision=HIGHEST, preferred_element_type=F32
    )
    wk_ref[...] = jnp.zeros_like(wk_ref)
    dense_ref[...] = jnp.zeros_like(dense_ref)
    wk_ref[2 * PARTS] = small
    pieces = jnp.concatenate([p.astype(F32) for p in split(base, 3)], axis=0).astype(BF16)
    for r in range(2):
        part = three_sum(
            jnp.dot(pieces[:, r * TILE : (r + 1) * TILE], tiles_ref[r], preferred_element_type=F32)
        )
        for j in range(NB):
            at = slice(j * TILE, (j + 1) * TILE)
            col = cols_ref[r, j]
            wk_ref[col] = wk_ref[col] + part[:, at]
            where = pl.ds(pl.multiple_of(arrival(place_ref, col) * TILE, TILE), TILE)
            dense_ref[r * TILE : (r + 1) * TILE, where] = tiles_ref[r, :, at]
    copy = pltpu.make_async_copy(wk_ref, wk_out_ref, sem)
    copy.start()
    copy.wait()


def step_rows(rate, z_speed):
    keep = 1.0 / (1.0 + rate)
    rows = [KERNEL_STEP * keep, rate * keep, 1.0 + rate, jnp.full((1, CELLS), z_speed)]
    return jnp.concatenate(rows + [jnp.zeros((4, CELLS), F32)], axis=0)


def base_kernel(z_ref, state_ref, rate_ref, weight_ref, above_ref, below_ref, base_ref):
    z_speed = z_ref[0]
    rate = rate_ref[...]
    keep = 1.0 / (1.0 + rate)
    for m in range(Q):
        half = slice(8 * m, 8 * m + 8)
        s = load_state(state_ref, m)
        e = advected_rows(m, s, below_ref[half, :], above_ref[half, :], z_speed)
        base_ref[Q * m : Q * m + Q, :] = keep * e
    base_ref[NODES:, :] = step_rows(rate, z_speed)
    base_ref[NODES + 4 : NODES + 5, :] = weight_ref[...]


def kernel_product(dense_ref, bundle_refs, stride):
    total = None
    for i, ref in enumerate(bundle_refs):
        blocks = [ref[j * stride : j * stride + NODES, :] for j in range(SIDE)]
        at = slice(i * SIDE * NODES, (i + 1) * SIDE * NODES)
        part = jnp.dot(
            dense_ref[:, at], jnp.concatenate(blocks, axis=0), preferred_element_type=F32
        )
        total = part if total is None else total + part
    return total


def first_kernel(
    dense_ref, base_ref, own_ref, near_ref, far_ref, back_ref, wk_in_ref,
    scaled_ref, payload_ref, wk_ref, sem,
):
    copy = pltpu.make_async_copy(wk_in_ref, wk_ref, sem)
    copy.start()
    term = kernel_product(dense_ref, (own_ref, near_ref, far_ref, back_ref), NODES)
    scaled = base_ref[0:NODES, :] + base_ref[NODES : NODES + 1, :] * term
    scaled_ref[0:NODES, :] = scaled
    scaled_ref[NODES : NODES + 8, :] = base_ref[NODES:, :]
    rows = base_ref[NODES:, :]
    _, _, phi = weights_rows(rows[3:4], rows[4:5])
    moments = jnp.dot(phi, scaled, precision=HIGHEST, preferred_element_type=F32)
    group = [moments[8 * t : 8 * t + 8] for t in range(GROUPS)]
    flux = group[1] + group[2]
    for t, shift in ((3, from_below_y), (4, from_above_y), (5, from_below_z), (6, from_above_z)):
        flux = flux + (group[t] - shift(group[t]))
    scaled_ref[NODES + 8 :, :] = flux
    k = iota((8, CELLS), 0)
    first = group[0]
    second = jnp.where(k < 5, group[1], pltpu.roll(group[2], 6, 0))
    copy.wait()
    small = jnp.concatenate([wk_ref[2 * PARTS], jnp.zeros((8, CELLS - TILE), F32)], axis=1)
    third = jnp.where(k < 5, small, pltpu.roll(group[2], 3, 0))
    for part in range(PARTS):
        wk = jnp.concatenate([wk_ref[2 * part], wk_ref[2 * part + 1]], axis=1)
        start = part * PAYLOAD
        payload_ref[start : start + 8, :] = jnp.where(k < 5, first, pltpu.roll(wk, 5, 0))
        payload_ref[start + 8 : start + 16, :] = jnp.where(
            (k < 5) | (k == 7), second, pltpu.roll(wk, 2, 0)
        )
        payload_ref[start + 16 : start + 24, :] = third


def totals_of(payload_ref, scaled_ref):
    total = payload_ref[0:PAYLOAD, :]
    for part in range(1, PARTS):
        total = total + payload_ref[part * PAYLOAD : (part + 1) * PAYLOAD, :]
    first, second, third = total[0:8], total[8:16], total[16:24]
    k = iota((8, CELLS), 0)
    mine = k < 5
    wk = jnp.where(k < 3, pltpu.roll(first, 3, 0), jnp.where(mine, pltpu.roll(second, 6, 0), 0.0))
    down = jnp.where(k == 1, pltpu.roll(second, 2, 0), jnp.where(mine, pltpu.roll(third, 5, 0), 0.0))
    down = jnp.where(k == 0, second - COURANT_SCALE * pltpu.roll(first, 7, 0), down)
    first, second, small = [jnp.where(mine, g, 0.0) for g in (first, second, third)]
    inverse = inverse_of(small[:, 0:128])
    rows = scaled_ref[NODES : NODES + 8, :]
    coeffs = rows[1:2] * apply_small(inverse, 8, rows[2:3] * first)
    return (first, second, down), wk, small, inverse, coeffs


def middle_kernel(payload_ref, scaled_ref, copies_ref, block_ref):
    group, wk, small, inverse, coeffs = totals_of(payload_ref, scaled_ref)
    z_speed = scaled_ref[NODES + 3 : NODES + 4, :]
    for m in range(Q):
        rows = slice(Q * m, Q * m + Q)
        s = scaled_ref[rows, :] + equilibrium_rows(m, coeffs, z_speed)
        rounded = s.astype(BF16)
        block_ref[rows, :] = rounded
        for part in range(SIDE):
            start = part * (NODES + EXTRA) + Q * m
            copies_ref[start : start + Q, :] = rounded
    pieces = jnp.concatenate([p.astype(F32) for p in split(wk, 3)], axis=0).astype(BF16)
    own = KERNEL_STEP * three_sum(jnp.dot(pieces, block_ref[...], preferred_element_type=F32))
    own = own - scaled_ref[NODES + 8 :, :]
    own = jnp.concatenate([p.astype(F32) for p in split(own, 2)], axis=0).astype(BF16)
    for part in range(SIDE):
        start = part * (NODES + EXTRA) + NODES
        copies_ref[start : start + EXTRA, :] = own


def state_kernel(payload_ref, scaled_ref, state_ref, low_ref, high_ref):
    group, wk, small, inverse, coeffs = totals_of(payload_ref, scaled_ref)
    z_speed = scaled_ref[NODES + 3 : NODES + 4, :]
    from_eq = [apply_small(small, 8 * t, coeffs) for t in range(GROUPS)]
    flux = from_eq[1] + from_eq[2]
    for t, shift in ((3, from_below_y), (4, from_above_y), (5, from_below_z), (6, from_above_z)):
        flux = flux + (from_eq[t] - shift(from_eq[t]))
    high_ref[NODES // 2 :, :] = group[1] + from_eq[1]
    low_ref[NODES // 2 :, :] = group[2] + from_eq[2]
    for m in range(Q):
        rows = slice(Q * m, Q * m + Q)
        s = scaled_ref[rows, :] + equilibrium_rows(m, coeffs, z_speed)
        state_ref[rows, :] = s
        store_sides(m, s, low_ref, high_ref)
    state_ref[NODES : NODES + 8, :] = group[0] + from_eq[0] - flux
    state_ref[NODES + 8 :, :] = jnp.concatenate([inverse, inverse], axis=1)


def second_base_kernel(z_ref, state_ref, rate_ref, above_ref, below_ref, base_ref):
    z_speed = z_ref[0]
    rate = rate_ref[...]
    keep = 1.0 / (1.0 + rate)
    for m in range(Q):
        rows = slice(Q * m, Q * m + Q)
        half = slice(8 * m, 8 * m + 8)
        e = advected_rows(m, state_ref[rows, :], below_ref[half, :], above_ref[half, :], z_speed)
        base_ref[rows, :] = keep * e
    sides_part = above_ref[NODES // 2 :, :] + below_ref[NODES // 2 :, :]
    base_ref[NODES : NODES + 8, :] = state_ref[NODES : NODES + 8, :] + sides_part
    base_ref[NODES + 8 : NODES + 16, :] = state_ref[NODES + 8 : NODES + 16, :]
    base_ref[NODES + 16 :, :] = step_rows(rate, z_speed)


def last_kernel(dense_ref, base_ref, own_ref, near_ref, far_ref, back_ref, out_ref, term_ref, new_ref, sems):
    stride = NODES + EXTRA
    bundles = (own_ref, near_ref, far_ref, back_ref)
    term_ref[...] = kernel_product(dense_ref, bundles, stride)
    total = base_ref[NODES : NODES + 8, :]
    for ref in bundles:
        for j in range(SIDE):
            own = ref[j * stride + NODES : (j + 1) * stride, :].astype(F32)
            total = total + (own[0:8] + own[8:16])
    rows = base_ref[NODES + 16 :, :]
    coeffs = rows[1:2] * apply_small(base_ref[NODES + 8 : NODES + 16, 0:128], 8, total)
    copies = []
    for m in range(Q):
        at = slice(Q * m, Q * m + Q)
        new = base_ref[at, :] + rows[0:1] * term_ref[at, :] + equilibrium_rows(m, coeffs, rows[3:4])
        for h in range(2):
            new_ref[pl.ds(2 * Q * m + h, Q, stride=2), :] = new[:, 128 * h : 128 * h + 128]
        if m % OUT_STEP == OUT_STEP - 1:
            at = slice(2 * Q * (m + 1 - OUT_STEP), 2 * Q * (m + 1))
            copies.append(
                pltpu.make_async_copy(new_ref.at[at], out_ref.at[at], sems.at[m // OUT_STEP])
            )
            copies[-1].start()
    for copy in copies:
        copy.wait()


VMEM = pl.BlockSpec(memory_space=pltpu.VMEM)
SMEM = pl.BlockSpec(memory_space=pltpu.SMEM)
HBM = pl.BlockSpec(memory_space=pltpu.HBM)


def call(kernel, scalars, arrays, outs, scratch=(), in_hbm=(), from_hbm=()):
    from_hbm = [pltpu.with_memory_space_constraint(a, pltpu.HBM) for a in from_hbm]
    return pl.pallas_call(
        kernel,
        out_shape=[
            (pltpu.HBM if i in in_hbm else jax.ShapeDtypeStruct)(shape, kind) for i, (shape, kind) in enumerate(outs)
        ],
        in_specs=[SMEM] * len(scalars) + [VMEM] * len(arrays) + [HBM] * len(from_hbm),
        out_specs=[HBM if i in in_hbm else VMEM for i in range(len(outs))],
        scratch_shapes=list(scratch),
        compiler_params=pltpu.CompilerParams(vmem_limit_bytes=VMEM_BYTES),
    )(*scalars, *arrays, *from_hbm)


def sides(low, high):
    count = lax.axis_size("gx")
    up = [(i, (i + 1) % count) for i in range(count)]
    down = [(target, source) for source, target in up]
    return lax.ppermute(low, "gx", down), lax.ppermute(high, "gx", up)


def spread(copies):
    return lax.all_to_all(copies, "vert", 0, 0, tiled=True)


def gather(copies):
    slabs = lax.axis_size("gx")
    groups, pairs = [], [[], [], []]
    for g in range(slabs):
        for i in range(SIDE):
            line = [i * SIDE + j if g % 2 == 1 else j * SIDE + i for j in range(SIDE)]
            groups.append([g * PARTS + v for v in line])
            for j in range(SIDE):
                for shift in (1, 2, 3):
                    y, x = (i + shift) % SIDE, j
                    ends = (i * SIDE + j, y * SIDE + x) if g % 2 == 1 else (j * SIDE + i, x * SIDE + y)
                    pairs[shift - 1].append(tuple(g * PARTS + v for v in ends))
    axes = ("gx", "vert")
    bundle = lax.all_to_all(copies, axes, 0, 0, axis_index_groups=groups, tiled=True)
    return [bundle] + [lax.ppermute(bundle, axes, p) for p in pairs]


def per_device(distribution, relax_rate, node_weight, kernel_tiles, tile_cols):
    state = distribution.reshape(2 * NODES, CELLS // 2)
    weight = node_weight.reshape(1, NODES)
    z_speed = speed_of(lax.axis_index("vert")).reshape(1)
    half = NODES // 2
    vert = lax.axis_index("vert")
    place = jnp.stack([1 - lax.axis_index("gx") % 2, vert // SIDE, vert % SIDE]).astype(jnp.int32)
    wk_rows = (2 * PARTS + 1, 8, TILE)
    dma = pltpu.SemaphoreType.DMA
    copies, low, high = call(
        copies_kernel, [], [state],
        [((SIDE * NODES, CELLS), BF16), ((half, CELLS), F32), ((half, CELLS), F32)],
    )
    bundles = gather(copies)
    dense, wk = call(
        prepare_kernel, [tile_cols, place, z_speed], [weight, kernel_tiles],
        [((NODES, PARTS * NODES), BF16), (wk_rows, F32)], [pltpu.VMEM(wk_rows, F32), dma], (1,),
    )
    above, below = sides(low, high)
    (base,) = call(
        base_kernel, [z_speed], [state, relax_rate, weight, above, below], [((NODES + 8, CELLS), F32)]
    )
    scaled, payload = call(
        first_kernel, [], [dense, base, *bundles],
        [((NODES + 16, CELLS), F32), ((PARTS * PAYLOAD, CELLS), F32)],
        [pltpu.VMEM(wk_rows, F32), dma], (), [wk],
    )
    payload = spread(payload)
    (copies,) = call(
        middle_kernel, [], [payload, scaled], [((SIDE * (NODES + EXTRA), CELLS), BF16)],
        [pltpu.VMEM((NODES, CELLS), BF16)],
    )
    bundles = gather(copies)
    state, low, high = call(
        state_kernel, [], [payload, scaled],
        [((NODES + 16, CELLS), F32), ((half + 8, CELLS), F32), ((half + 8, CELLS), F32)],
    )
    above, below = sides(low, high)
    (base,) = call(
        second_base_kernel, [z_speed], [state, relax_rate, above, below],
        [((NODES + 24, CELLS), F32)],
    )
    (out,) = call(
        last_kernel, [], [dense, base, *bundles], [((2 * NODES, CELLS // 2), F32)],
        [
            pltpu.VMEM((NODES, CELLS), F32), pltpu.VMEM((2 * NODES, CELLS // 2), F32),
            pltpu.SemaphoreType.DMA((Q // OUT_STEP,)),
        ],
        (0,),
    )
    return out.reshape(distribution.shape)


def solution(mesh):
    placed = (
        P("vert", "gx", None),
        P("gx", None),
        P("vert"),
        P("vert", None, None),
        P("vert", None),
    )
    return jax.shard_map(
        per_device, mesh=mesh, in_specs=placed, out_specs=P("vert", "gx", None), check_vma=False
    )
```

```python
import functools

import jax
import jax.numpy as jnp
from jax import lax
from jax.experimental import pallas as pl
from jax.experimental.pallas import tpu as pltpu
from jax.sharding import PartitionSpec as P

Q = 16
TILE = 128
NB = 12
NZ = 4
CELLS = 256
NODES = 256
PARTS = 16
COURANT_SCALE = 0.3
KERNEL_STEP = 0.5
MIDDLE = (Q - 1) / 2.0
EXTRA = 16
PAYLOAD = 24
SIDE = 4
GROUPS = 7
F32 = jnp.float32
BF16 = jnp.bfloat16
HIGHEST = lax.Precision.HIGHEST
VMEM_BYTES = 24 * 1024 * 1024


def iota(shape, dim):
    return lax.broadcasted_iota(jnp.int32, shape, dim)


def speed_of(index):
    return (index.astype(F32) - MIDDLE) / MIDDLE


def from_below_y(a):
    return pltpu.roll(a, NZ, 1)


def from_above_y(a):
    return pltpu.roll(a, CELLS - NZ, 1)


def from_below_z(a):
    first = iota(a.shape, 1) % NZ == 0
    return jnp.where(first, pltpu.roll(a, CELLS - (NZ - 1), 1), pltpu.roll(a, 1, 1))


def from_above_z(a):
    last = iota(a.shape, 1) % NZ == NZ - 1
    return jnp.where(last, pltpu.roll(a, NZ - 1, 1), pltpu.roll(a, CELLS - 1, 1))


def split(a, pieces):
    out = []
    for _ in range(pieces):
        out.append(a.astype(BF16))
        a = a - out[-1].astype(F32)
    return out


def three_sum(a):
    return a[0:8] + a[8:16] + a[16:24]


def node_rows(z_speed):
    node = iota((8, NODES), 1)
    k = iota((8, NODES), 0)
    x, y = speed_of(node % Q), speed_of(node // Q)
    z = jnp.broadcast_to(z_speed, (8, NODES))
    invariants = jnp.where(k == 0, 1.0, 0.0)
    for row, value in ((1, x), (2, y), (3, z), (4, x * x + y * y + z * z)):
        invariants = jnp.where(k == row, value, invariants)
    factors = [None]
    for speed in (x, y, z):
        factors.append(COURANT_SCALE * jnp.maximum(speed, 0.0))
        factors.append(COURANT_SCALE * jnp.maximum(-speed, 0.0))
    return invariants, factors


def weights_rows(z_speed, weight):
    invariants, factors = node_rows(z_speed)
    base = weight * invariants
    return invariants, base, jnp.concatenate([base] + [base * f for f in factors[1:]], axis=0)


def advected_rows(m, s, below, above, z_speed):
    row = iota((Q, CELLS), 0)
    lane = iota((Q, CELLS), 1)
    x_courant = COURANT_SCALE * jnp.abs(speed_of(row))
    y_courant = COURANT_SCALE * abs((m - MIDDLE) / MIDDLE)
    z_courant = COURANT_SCALE * jnp.abs(z_speed)
    up = z_speed > 0
    edge = jnp.where(up, 0, NZ - 1)
    near = pltpu.roll(s, jnp.where(up, 1, CELLS - 1), 1)
    far = pltpu.roll(s, jnp.where(up, CELLS - (NZ - 1), NZ - 1), 1)
    z_side = jnp.where(lane % NZ == edge, far, near)
    y_side = from_below_y(s) if m >= Q // 2 else from_above_y(s)
    x_side = jnp.concatenate([above, below], axis=0)
    flux = x_courant * (s - x_side) + y_courant * (s - y_side) + z_courant * (s - z_side)
    return s - flux


def equilibrium_rows(m, coeffs, z_speed):
    y = (m - MIDDLE) / MIDDLE
    x = speed_of(iota((Q, CELLS), 0))
    common = coeffs[0:1] + y * coeffs[2:3] + z_speed * coeffs[3:4]
    common = common + (y * y + z_speed * z_speed) * coeffs[4:5]
    return common + x * coeffs[1:2] + (x * x) * coeffs[4:5]


def apply_small(matrix, first, rows):
    total = matrix[:, first : first + 1] * rows[0:1]
    for k in range(1, 5):
        total = total + matrix[:, first + k : first + k + 1] * rows[k : k + 1]
    return total


def inverse_of(gram):
    row, lane = iota((8, 128), 0), iota((8, 128), 1)
    work = jnp.where((row < 5) & (lane < 5), gram, 0.0)
    work = jnp.where((lane == row + 8) | ((lane == row) & (row >= 5)), 1.0, work)
    for i in range(5):
        pivot = work[i : i + 1, :] / work[i : i + 1, i : i + 1]
        work = jnp.where(row == i, pivot, work - work[:, i : i + 1] * pivot)
    return work


def load_state(ref, m):
    halves = [ref[pl.ds(2 * Q * m + h, Q, stride=2), :] for h in range(2)]
    return jnp.concatenate(halves, axis=1)


def store_sides(m, s, low_ref, high_ref):
    low_ref[8 * m : 8 * m + 8, :] = s[0:8]
    high_ref[8 * m : 8 * m + 8, :] = s[8:16]


def copies_kernel(state_ref, copies_ref, low_ref, high_ref):
    for m in range(Q):
        s = load_state(state_ref, m)
        store_sides(m, s, low_ref, high_ref)
        rounded = s.astype(BF16)
        for part in range(SIDE):
            copies_ref[part * NODES + Q * m : part * NODES + Q * m + Q, :] = rounded


def arrival(place_ref, col):
    first, y, x = place_ref[0], place_ref[1], place_ref[2]
    from_y, from_x = col // (2 * SIDE), col // 2 % SIDE
    bundle = jnp.where(first == 0, y - from_y, x - from_x)
    bundle = jnp.where(bundle < 0, bundle + SIDE, bundle)
    return (bundle * SIDE + jnp.where(first == 0, from_x, from_y)) * 2 + col % 2


def prepare_kernel(
    cols_ref, place_ref, z_ref, weight_ref, tiles_ref, dense_ref, wk_out_ref, wk_ref, sem
):
    invariants, base, phi = weights_rows(z_ref[0], weight_ref[...])
    padded = jnp.concatenate([phi, jnp.zeros((TILE - 8 * GROUPS, NODES), F32)], axis=0)
    small = lax.dot_general(
        invariants, padded, (((1,), (1,)), ((), ())), precision=HIGHEST, preferred_element_type=F32
    )
    wk_ref[...] = jnp.zeros_like(wk_ref)
    dense_ref[...] = jnp.zeros_like(dense_ref)
    wk_ref[2 * PARTS] = small
    pieces = jnp.concatenate([p.astype(F32) for p in split(base, 3)], axis=0).astype(BF16)
    for r in range(2):
        part = three_sum(
            jnp.dot(pieces[:, r * TILE : (r + 1) * TILE], tiles_ref[r], preferred_element_type=F32)
        )
        for j in range(NB):
            at = slice(j * TILE, (j + 1) * TILE)
            col = cols_ref[r, j]
            wk_ref[col] = wk_ref[col] + part[:, at]
            where = pl.ds(pl.multiple_of(arrival(place_ref, col) * TILE, TILE), TILE)
            dense_ref[r * TILE : (r + 1) * TILE, where] = tiles_ref[r, :, at]
    copy = pltpu.make_async_copy(wk_ref, wk_out_ref, sem)
    copy.start()
    copy.wait()


def step_rows(rate, z_speed):
    keep = 1.0 / (1.0 + rate)
    rows = [KERNEL_STEP * keep, rate * keep, 1.0 + rate, jnp.full((1, CELLS), z_speed)]
    return jnp.concatenate(rows + [jnp.zeros((4, CELLS), F32)], axis=0)


def base_kernel(z_ref, state_ref, rate_ref, weight_ref, above_ref, below_ref, base_ref):
    z_speed = z_ref[0]
    rate = rate_ref[...]
    keep = 1.0 / (1.0 + rate)
    for m in range(Q):
        half = slice(8 * m, 8 * m + 8)
        s = load_state(state_ref, m)
        e = advected_rows(m, s, below_ref[half, :], above_ref[half, :], z_speed)
        base_ref[Q * m : Q * m + Q, :] = keep * e
    base_ref[NODES:, :] = step_rows(rate, z_speed)
    base_ref[NODES + 4 : NODES + 5, :] = weight_ref[...]


def kernel_product(dense_ref, bundle_refs, stride):
    total = None
    for i, ref in enumerate(bundle_refs):
        blocks = [ref[j * stride : j * stride + NODES, :] for j in range(SIDE)]
        at = slice(i * SIDE * NODES, (i + 1) * SIDE * NODES)
        part = jnp.dot(
            dense_ref[:, at], jnp.concatenate(blocks, axis=0), preferred_element_type=F32
        )
        total = part if total is None else total + part
    return total


def first_kernel(
    dense_ref, base_ref, own_ref, near_ref, far_ref, back_ref, wk_in_ref,
    scaled_ref, payload_ref, wk_ref, sem,
):
    copy = pltpu.make_async_copy(wk_in_ref, wk_ref, sem)
    copy.start()
    term = kernel_product(dense_ref, (own_ref, near_ref, far_ref, back_ref), NODES)
    scaled = base_ref[0:NODES, :] + base_ref[NODES : NODES + 1, :] * term
    scaled_ref[0:NODES, :] = scaled
    scaled_ref[NODES : NODES + 8, :] = base_ref[NODES:, :]
    rows = base_ref[NODES:, :]
    _, _, phi = weights_rows(rows[3:4], rows[4:5])
    moments = jnp.dot(phi, scaled, precision=HIGHEST, preferred_element_type=F32)
    group = [moments[8 * t : 8 * t + 8] for t in range(GROUPS)]
    flux = group[1] + group[2]
    for t, shift in ((3, from_below_y), (4, from_above_y), (5, from_below_z), (6, from_above_z)):
        flux = flux + (group[t] - shift(group[t]))
    scaled_ref[NODES + 8 :, :] = flux
    k = iota((8, CELLS), 0)
    first = group[0]
    second = jnp.where(k < 5, group[1], pltpu.roll(group[2], 6, 0))
    copy.wait()
    small = jnp.concatenate([wk_ref[2 * PARTS], jnp.zeros((8, CELLS - TILE), F32)], axis=1)
    third = jnp.where(k < 5, small, pltpu.roll(group[2], 3, 0))
    for part in range(PARTS):
        wk = jnp.concatenate([wk_ref[2 * part], wk_ref[2 * part + 1]], axis=1)
        start = part * PAYLOAD
        payload_ref[start : start + 8, :] = jnp.where(k < 5, first, pltpu.roll(wk, 5, 0))
        payload_ref[start + 8 : start + 16, :] = jnp.where(
            (k < 5) | (k == 7), second, pltpu.roll(wk, 2, 0)
        )
        payload_ref[start + 16 : start + 24, :] = third


def totals_of(payload_ref, scaled_ref):
    total = payload_ref[0:PAYLOAD, :]
    for part in range(1, PARTS):
        total = total + payload_ref[part * PAYLOAD : (part + 1) * PAYLOAD, :]
    first, second, third = total[0:8], total[8:16], total[16:24]
    k = iota((8, CELLS), 0)
    mine = k < 5
    wk = jnp.where(k < 3, pltpu.roll(first, 3, 0), jnp.where(mine, pltpu.roll(second, 6, 0), 0.0))
    down = jnp.where(k == 1, pltpu.roll(second, 2, 0), jnp.where(mine, pltpu.roll(third, 5, 0), 0.0))
    down = jnp.where(k == 0, second - COURANT_SCALE * pltpu.roll(first, 7, 0), down)
    first, second, small = [jnp.where(mine, g, 0.0) for g in (first, second, third)]
    inverse = inverse_of(small[:, 0:128])
    rows = scaled_ref[NODES : NODES + 8, :]
    coeffs = rows[1:2] * apply_small(inverse, 8, rows[2:3] * first)
    return (first, second, down), wk, small, inverse, coeffs


def middle_kernel(
    payload_ref, scaled_ref, copies_ref, state_ref, low_ref, high_ref, block_ref
):
    group, wk, small, inverse, coeffs = totals_of(payload_ref, scaled_ref)
    z_speed = scaled_ref[NODES + 3 : NODES + 4, :]
    for m in range(Q):
        rows = slice(Q * m, Q * m + Q)
        s = scaled_ref[rows, :] + equilibrium_rows(m, coeffs, z_speed)
        state_ref[rows, :] = s
        store_sides(m, s, low_ref, high_ref)
        rounded = s.astype(BF16)
        block_ref[rows, :] = rounded
        for part in range(SIDE):
            start = part * (NODES + EXTRA) + Q * m
            copies_ref[start : start + Q, :] = rounded
    pieces = jnp.concatenate([p.astype(F32) for p in split(wk, 3)], axis=0).astype(BF16)
    own = KERNEL_STEP * three_sum(jnp.dot(pieces, block_ref[...], preferred_element_type=F32))
    own = own - scaled_ref[NODES + 8 :, :]
    own = jnp.concatenate([p.astype(F32) for p in split(own, 2)], axis=0).astype(BF16)
    for part in range(SIDE):
        start = part * (NODES + EXTRA) + NODES
        copies_ref[start : start + EXTRA, :] = own
    from_eq = [apply_small(small, 8 * t, coeffs) for t in range(GROUPS)]
    flux = from_eq[1] + from_eq[2]
    for t, shift in ((3, from_below_y), (4, from_above_y), (5, from_below_z), (6, from_above_z)):
        flux = flux + (from_eq[t] - shift(from_eq[t]))
    high_ref[NODES // 2 :, :] = group[1] + from_eq[1]
    low_ref[NODES // 2 :, :] = group[2] + from_eq[2]
    state_ref[NODES : NODES + 8, :] = group[0] + from_eq[0] - flux
    state_ref[NODES + 8 :, :] = jnp.concatenate([inverse, inverse], axis=1)


def second_base_kernel(z_ref, state_ref, rate_ref, above_ref, below_ref, base_ref):
    z_speed = z_ref[0]
    rate = rate_ref[...]
    keep = 1.0 / (1.0 + rate)
    for m in range(Q):
        rows = slice(Q * m, Q * m + Q)
        half = slice(8 * m, 8 * m + 8)
        e = advected_rows(m, state_ref[rows, :], below_ref[half, :], above_ref[half, :], z_speed)
        base_ref[rows, :] = keep * e
    sides_part = above_ref[NODES // 2 :, :] + below_ref[NODES // 2 :, :]
    base_ref[NODES : NODES + 8, :] = state_ref[NODES : NODES + 8, :] + sides_part
    base_ref[NODES + 8 : NODES + 16, :] = state_ref[NODES + 8 : NODES + 16, :]
    base_ref[NODES + 16 :, :] = step_rows(rate, z_speed)


def last_kernel(dense_ref, base_ref, own_ref, near_ref, far_ref, back_ref, out_ref, term_ref):
    stride = NODES + EXTRA
    bundles = (own_ref, near_ref, far_ref, back_ref)
    term_ref[...] = kernel_product(dense_ref, bundles, stride)
    total = base_ref[NODES : NODES + 8, :]
    for ref in bundles:
        for j in range(SIDE):
            own = ref[j * stride + NODES : (j + 1) * stride, :].astype(F32)
            total = total + (own[0:8] + own[8:16])
    rows = base_ref[NODES + 16 :, :]
    coeffs = rows[1:2] * apply_small(base_ref[NODES + 8 : NODES + 16, 0:128], 8, total)
    for m in range(Q):
        at = slice(Q * m, Q * m + Q)
        new = base_ref[at, :] + rows[0:1] * term_ref[at, :] + equilibrium_rows(m, coeffs, rows[3:4])
        for h in range(2):
            out_ref[pl.ds(2 * Q * m + h, Q, stride=2), :] = new[:, 128 * h : 128 * h + 128]


VMEM = pl.BlockSpec(memory_space=pltpu.VMEM)
SMEM = pl.BlockSpec(memory_space=pltpu.SMEM)
HBM = pl.BlockSpec(memory_space=pltpu.HBM)


def call(kernel, scalars, arrays, outs, scratch=(), in_hbm=(), from_hbm=()):
    from_hbm = [pltpu.with_memory_space_constraint(a, pltpu.HBM) for a in from_hbm]
    return pl.pallas_call(
        kernel,
        out_shape=[
            (pltpu.HBM if i in in_hbm else jax.ShapeDtypeStruct)(shape, kind) for i, (shape, kind) in enumerate(outs)
        ],
        in_specs=[SMEM] * len(scalars) + [VMEM] * len(arrays) + [HBM] * len(from_hbm),
        out_specs=[HBM if i in in_hbm else VMEM for i in range(len(outs))],
        scratch_shapes=list(scratch),
        compiler_params=pltpu.CompilerParams(vmem_limit_bytes=VMEM_BYTES),
    )(*scalars, *arrays, *from_hbm)


def sides(low, high):
    count = lax.axis_size("gx")
    up = [(i, (i + 1) % count) for i in range(count)]
    down = [(target, source) for source, target in up]
    return lax.ppermute(low, "gx", down), lax.ppermute(high, "gx", up)


def spread(copies):
    return lax.all_to_all(copies, "vert", 0, 0, tiled=True)


def gather(copies):
    slabs = lax.axis_size("gx")
    groups, pairs = [], [[], [], []]
    for g in range(slabs):
        for i in range(SIDE):
            line = [i * SIDE + j if g % 2 == 1 else j * SIDE + i for j in range(SIDE)]
            groups.append([g * PARTS + v for v in line])
            for j in range(SIDE):
                for shift in (1, 2, 3):
                    y, x = (i + shift) % SIDE, j
                    ends = (i * SIDE + j, y * SIDE + x) if g % 2 == 1 else (j * SIDE + i, x * SIDE + y)
                    pairs[shift - 1].append(tuple(g * PARTS + v for v in ends))
    axes = ("gx", "vert")
    bundle = lax.all_to_all(copies, axes, 0, 0, axis_index_groups=groups, tiled=True)
    return [bundle] + [lax.ppermute(bundle, axes, p) for p in pairs]


def per_device(distribution, relax_rate, node_weight, kernel_tiles, tile_cols):
    state = distribution.reshape(2 * NODES, CELLS // 2)
    weight = node_weight.reshape(1, NODES)
    z_speed = speed_of(lax.axis_index("vert")).reshape(1)
    half = NODES // 2
    vert = lax.axis_index("vert")
    place = jnp.stack([1 - lax.axis_index("gx") % 2, vert // SIDE, vert % SIDE]).astype(jnp.int32)
    wk_rows = (2 * PARTS + 1, 8, TILE)
    dma = pltpu.SemaphoreType.DMA
    copies, low, high = call(
        copies_kernel, [], [state],
        [((SIDE * NODES, CELLS), BF16), ((half, CELLS), F32), ((half, CELLS), F32)],
    )
    bundles = gather(copies)
    dense, wk = call(
        prepare_kernel, [tile_cols, place, z_speed], [weight, kernel_tiles],
        [((NODES, PARTS * NODES), BF16), (wk_rows, F32)], [pltpu.VMEM(wk_rows, F32), dma], (1,),
    )
    above, below = sides(low, high)
    (base,) = call(
        base_kernel, [z_speed], [state, relax_rate, weight, above, below], [((NODES + 8, CELLS), F32)]
    )
    scaled, payload = call(
        first_kernel, [], [dense, base, *bundles],
        [((NODES + 16, CELLS), F32), ((PARTS * PAYLOAD, CELLS), F32)],
        [pltpu.VMEM(wk_rows, F32), dma], (), [wk],
    )
    payload = spread(payload)
    copies, state, low, high = call(
        middle_kernel, [], [payload, scaled],
        [
            ((SIDE * (NODES + EXTRA), CELLS), BF16), ((NODES + 16, CELLS), F32),
            ((half + 8, CELLS), F32), ((half + 8, CELLS), F32),
        ],
        [pltpu.VMEM((NODES, CELLS), BF16)],
    )
    bundles = gather(copies)
    above, below = sides(low, high)
    (base,) = call(
        second_base_kernel, [z_speed], [state, relax_rate, above, below],
        [((NODES + 24, CELLS), F32)],
    )
    (out,) = call(
        last_kernel, [], [dense, base, *bundles], [((2 * NODES, CELLS // 2), F32)],
        [pltpu.VMEM((NODES, CELLS), F32)],
    )
    return out.reshape(distribution.shape)


def solution(mesh):
    placed = (
        P("vert", "gx", None),
        P("gx", None),
        P("vert"),
        P("vert", None, None),
        P("vert", None),
    )
    return jax.shard_map(
        per_device, mesh=mesh, in_specs=placed, out_specs=P("vert", "gx", None), check_vma=False
    )
```
